32 devices in a mesh: dp: 4 (over z), adapter: 2 (over x), tensor: 4 (over y, core).
Axes of the slice: x: 2, y: 2, z: 4, core: 2. Of those that a mesh axis runs over, the one named last changes fastest.
Arguments:
- tokens: bfloat16 [6144, 8192], P(('dp', 'adapter'), 'tensor'), may hold values from -6 to 6
- frozen_value_weight: bfloat16 [8192, 1024], P('tensor'), may hold values from -0.0625 to 0.0625
- adapter_down_weight: bfloat16 [24, 64, 8192], P(('adapter', 'tensor')), may hold values from -0.0625 to 0.0625
- adapter_up_weight: bfloat16 [24, 64, 1024], P(('adapter', 'tensor')), may hold values from -0.75 to 0.75
- cotangent: bfloat16 [6144, 1024], P(('dp', 'adapter')), may hold values from -12 to 12
- language_pair_index: int32 [6144], P(('dp', 'adapter')), may hold values from 0 to 23, as said below
- language_pair_counts: int32 [8, 24], P(('dp', 'adapter')), may hold values from 0 to 64, as said below
- adapter_owner_table: int32 [24], replicated, may hold values from 0 to 23, as said below
Outputs:
- mixed_out: bfloat16 [6144, 1024], P(('dp', 'adapter'), 'tensor')
- token_input_gradient: bfloat16 [6144, 8192], P(('dp', 'adapter'), 'tensor')
- grad_down: bfloat16 [24, 64, 8192], P(('adapter', 'tensor'), 'dp')
- grad_up: bfloat16 [24, 64, 1024], P(('adapter', 'tensor'), 'dp')
The draws below stay inside these ranges and needn't reach their ends.
Inputs may be any that keep to these rules, and one draw needn't show every extreme that they name: `language_pair_index`: within one row block (the 768 rows of one index of dp+adapter), at most 192 rows have pairs whose stored index adapter_owner_table[p] lies in one owner's range [o * 3, (o + 1) * 3); for each dp index one owner gets exactly 192 rows from every row block of that dp index. language_pair_counts[g, p] is the number of rows of row block g whose pair id is p; in every row block some pair has exactly (192 + 3 - 1) // 3 rows. `adapter_owner_table`: A permutation of 0 to 23.
All inputs are finite; a program needn't handle non-finite values.
Results may differ from the reference program's by a relative error of at most 0.012.
Values may be sent and summed in bfloat16 or wider, within the bound.
No kernel may reach another device: no remote copies, remote signals or barrier semaphores. Data moves between devices by JAX's collectives and lax.ppermute only.
A program may use at most 128 MiB of HBM per device.

```python
import jax
import jax.numpy as jnp
from jax import lax

MODEL_WIDTH = 8192
VALUE_OUTPUTS = 1024
ADAPTER_RANK = 64
ADP_DEV = 3
TOK_DEV = 768
OWNERS = 8
ROWGROUPS = 8
REPLICAS = 4
TOKENS = 6144
ADAPTER_COUNT = 24
CAP = 192


def routing_tables(key):
    adapter_owner_table = jax.random.permutation(jax.random.fold_in(key, 101), ADAPTER_COUNT).astype(jnp.int32)
    pair_of_slot = jnp.argsort(adapter_owner_table, stable=True).astype(jnp.int32)
    group_index = jnp.arange(ROWGROUPS, dtype=jnp.int32)
    hot_each = jax.random.randint(jax.random.fold_in(key, 102), (REPLICAS,), 0, OWNERS)
    hot_owner = hot_each[group_index // (ROWGROUPS // REPLICAS)]
    offset_owner = jax.random.randint(jax.random.fold_in(key, 103), (ROWGROUPS,), 0, OWNERS - 1)
    offset_local = jax.random.randint(jax.random.fold_in(key, 104), (ROWGROUPS,), 0, ADP_DEV)
    row_index = jnp.arange(TOK_DEV, dtype=jnp.int32)[None, :]
    spread_rows = jnp.maximum(row_index - CAP, 0) + offset_owner[:, None]
    in_hot = row_index < CAP
    owner_of = jnp.where(in_hot, hot_owner[:, None], (hot_owner[:, None] + 1 + spread_rows % (OWNERS - 1)) % OWNERS)
    rank_in_owner = jnp.where(in_hot, row_index, spread_rows // (OWNERS - 1))
    local_slot = (rank_in_owner + offset_local[:, None]) % ADP_DEV
    pair_grid = pair_of_slot[owner_of * ADP_DEV + local_slot]
    shuffle_keys = jax.random.split(jax.random.fold_in(key, 105), ROWGROUPS)
    shuffles = jax.vmap(jax.random.permutation, in_axes=(0, None))(shuffle_keys, TOK_DEV).astype(jnp.int32)
    pair_grid = jnp.take_along_axis(pair_grid, shuffles, axis=1).astype(jnp.int32)
    pair_table = jnp.arange(ADAPTER_COUNT, dtype=jnp.int32)
    counts_grid = jnp.sum((pair_grid[:, :, None] == pair_table[None, None, :]).astype(jnp.int32), axis=1).astype(jnp.int32)
    return (pair_grid.reshape(TOKENS), counts_grid, adapter_owner_table)


def draw_language_pair_index(key, part):
    return routing_tables(key)[0]


def draw_language_pair_counts(key, part):
    return routing_tables(key)[1]


def draw_adapter_owner_table(key, part):
    return routing_tables(key)[2]


def shard_levels(stream_key, dims, shards, low, high):
    loudness = 1.0
    for position, shards_of in shards:
        steps = jax.random.uniform(jax.random.fold_in(jax.random.fold_in(stream_key, 6), position), (shards_of,), jnp.float32, low / len(shards), high / len(shards))
        loudness = loudness * jnp.repeat(jnp.exp(steps), dims[position] // shards_of).reshape((-1,) + (1,) * (len(dims) - 1 - position))
    return loudness


def centred(rng, dims, scale, most, cuts=(), kind=jnp.bfloat16):
    result = jax.random.normal(rng, dims, jnp.float32) * scale
    if len(cuts) > 0:
        result = shard_levels(rng, dims, cuts, -0.22, 0.18) * result
    return jnp.clip(result, min=-most, max=most).astype(kind)


def setup_inputs(seed: int = 0) -> dict:
    seeds = jax.random.split(jax.random.key(seed), 9)
    tokens = centred(seeds[0], (TOKENS, MODEL_WIDTH), 1.0, 6.0, ((0, 8), (1, 4)))
    frozen_value_weight = centred(seeds[1], (MODEL_WIDTH, VALUE_OUTPUTS), MODEL_WIDTH ** -0.5, 0.0625, ((0, 4),))
    adapter_down_weight = centred(seeds[2], (ADAPTER_COUNT, ADAPTER_RANK, MODEL_WIDTH), MODEL_WIDTH ** -0.5, 0.0625, ((0, 8),))
    adapter_up_weight = centred(seeds[3], (ADAPTER_COUNT, ADAPTER_RANK, VALUE_OUTPUTS), ADAPTER_RANK ** -0.5, 0.75, ((0, 8),))
    cotangent = centred(seeds[4], (TOKENS, VALUE_OUTPUTS), 2.0, 12.0, ((0, 8),))
    language_pair_index = draw_language_pair_index(jax.random.fold_in(seeds[8], 71), 0)
    language_pair_counts = draw_language_pair_counts(jax.random.fold_in(seeds[8], 71), 0)
    adapter_owner_table = draw_adapter_owner_table(jax.random.fold_in(seeds[8], 71), 0)
    return {"tokens": tokens, "frozen_value_weight": frozen_value_weight, "adapter_down_weight": adapter_down_weight, "adapter_up_weight": adapter_up_weight, "cotangent": cotangent, "language_pair_index": language_pair_index, "language_pair_counts": language_pair_counts, "adapter_owner_table": adapter_owner_table}


ADAPTER_SCALE = 0.5
block_rows = 128


def grouped_adapter_forward(input_rows, gradient_rows, slot_index, adapter_down_weight, adapter_up_weight):
    total_rows = input_rows.shape[0]
    feature_width = input_rows.shape[1]
    value_width = gradient_rows.shape[1]
    row_order = jnp.argsort(slot_index, stable=True).astype(jnp.int32)
    sorted_x = jnp.concatenate([input_rows[row_order], jnp.zeros((block_rows, feature_width), input_rows.dtype)], axis=0)
    sorted_g = jnp.concatenate([gradient_rows[row_order], jnp.zeros((block_rows, value_width), gradient_rows.dtype)], axis=0)
    slot_table = jnp.arange(ADAPTER_COUNT, dtype=jnp.int32)
    per_slot = jnp.sum((slot_index[:, None] == slot_table[None, :]).astype(jnp.int32), axis=0).astype(jnp.int32)
    blocks_of = ((per_slot + block_rows - 1) // block_rows).astype(jnp.int32)
    block_first = (jnp.cumsum(blocks_of) - blocks_of).astype(jnp.int32)
    row_first = (jnp.cumsum(per_slot) - per_slot).astype(jnp.int32)
    block_total = total_rows // block_rows + 1 + ADAPTER_COUNT
    offsets = jnp.arange(block_rows, dtype=jnp.int32)
    initial = (
        jnp.zeros((total_rows + block_rows, value_width), jnp.bfloat16),
        jnp.zeros((total_rows + block_rows, feature_width), jnp.bfloat16),
        jnp.zeros((ADAPTER_COUNT, ADAPTER_RANK, feature_width), jnp.float32),
        jnp.zeros((ADAPTER_COUNT, ADAPTER_RANK, value_width), jnp.float32),
    )

    def advance(block_index, state_tuple):
        delta_sorted, input_sorted, down_total, up_weight_total = state_tuple
        block_index = jnp.asarray(block_index).astype(jnp.int32)
        selected_adapter = jnp.clip(jnp.sum((block_first <= block_index).astype(jnp.int32)) - 1, 0, ADAPTER_COUNT - 1).astype(jnp.int32)
        inner_block = (block_index - block_first[selected_adapter]).astype(jnp.int32)
        live_rows = (per_slot[selected_adapter] - inner_block * block_rows).astype(jnp.int32)
        first_row = jnp.clip(row_first[selected_adapter] + inner_block * block_rows, 0, total_rows).astype(jnp.int32)
        keep_rows = (offsets < live_rows)[:, None]
        block_x = lax.dynamic_slice_in_dim(sorted_x, first_row, block_rows, 0)
        block_gradient = lax.dynamic_slice_in_dim(sorted_g, first_row, block_rows, 0)
        down_weight_matrix = lax.dynamic_index_in_dim(adapter_down_weight, selected_adapter, 0, keepdims=False)
        up_weight_matrix = lax.dynamic_index_in_dim(adapter_up_weight, selected_adapter, 0, keepdims=False)
        reduced_activation = jnp.dot(block_x, down_weight_matrix.T, preferred_element_type=jnp.float32).astype(jnp.bfloat16)
        adapter_output_rows = (ADAPTER_SCALE * jnp.dot(reduced_activation, up_weight_matrix, preferred_element_type=jnp.float32)).astype(jnp.bfloat16)
        backward_activation = (ADAPTER_SCALE * jnp.dot(block_gradient, up_weight_matrix.T, preferred_element_type=jnp.float32)).astype(jnp.bfloat16)
        input_piece = jnp.dot(backward_activation, down_weight_matrix, preferred_element_type=jnp.float32).astype(jnp.bfloat16)
        reduced_saved = jnp.where(keep_rows, reduced_activation, jnp.zeros_like(reduced_activation))
        back_kept = jnp.where(keep_rows, backward_activation, jnp.zeros_like(backward_activation))
        old_delta = lax.dynamic_slice_in_dim(delta_sorted, first_row, block_rows, 0)
        delta_sorted = lax.dynamic_update_slice_in_dim(delta_sorted, jnp.where(keep_rows, adapter_output_rows, old_delta), first_row, 0)
        old_input = lax.dynamic_slice_in_dim(input_sorted, first_row, block_rows, 0)
        input_sorted = lax.dynamic_update_slice_in_dim(input_sorted, jnp.where(keep_rows, input_piece, old_input), first_row, 0)
        down_total = down_total.at[selected_adapter].add(jnp.dot(back_kept.T, block_x, preferred_element_type=jnp.float32))
        up_weight_total = up_weight_total.at[selected_adapter].add(ADAPTER_SCALE * jnp.dot(reduced_saved.T, block_gradient, preferred_element_type=jnp.float32))
        return (delta_sorted, input_sorted, down_total, up_weight_total)

    delta_sorted, input_sorted, down_total, up_weight_total = lax.fori_loop(0, block_total, advance, initial)
    adapter_output = jnp.zeros((total_rows, value_width), jnp.bfloat16).at[row_order].set(delta_sorted[:total_rows])
    input_out = jnp.zeros((total_rows, feature_width), jnp.bfloat16).at[row_order].set(input_sorted[:total_rows])
    return adapter_output, input_out, down_total, up_weight_total


def reference(tokens, frozen_value_weight, adapter_down_weight, adapter_up_weight, cotangent, language_pair_index, language_pair_counts, adapter_owner_table):
    slot_index = adapter_owner_table[language_pair_index].astype(jnp.int32)
    base = jnp.dot(tokens, frozen_value_weight, preferred_element_type=jnp.float32)
    group_of = (jnp.arange(TOKENS, dtype=jnp.int32) // TOK_DEV).astype(jnp.int32)
    row_weight = 1.0 / language_pair_counts[group_of, language_pair_index].astype(jnp.float32)
    scaled = (cotangent.astype(jnp.float32) * row_weight[:, None]).astype(jnp.bfloat16)
    frozen_gradient = jnp.dot(scaled, frozen_value_weight.T, preferred_element_type=jnp.float32)
    replica_share = TOKENS // REPLICAS
    delta_list = []
    input_collection = []
    down_sum = jnp.zeros((ADAPTER_COUNT, ADAPTER_RANK, MODEL_WIDTH), jnp.float32)
    up_sum = jnp.zeros((ADAPTER_COUNT, ADAPTER_RANK, VALUE_OUTPUTS), jnp.float32)
    for replica in range(REPLICAS):
        leading_row = replica * replica_share
        adapter_output_piece, input_piece, down_weight_piece, up_weight_piece = grouped_adapter_forward(
            tokens[leading_row:leading_row + replica_share], scaled[leading_row:leading_row + replica_share],
            slot_index[leading_row:leading_row + replica_share], adapter_down_weight, adapter_up_weight)
        delta_list.append(adapter_output_piece)
        input_collection.append(input_piece)
        down_round = lax.optimization_barrier(down_weight_piece.astype(jnp.bfloat16))
        up_round = lax.optimization_barrier(up_weight_piece.astype(jnp.bfloat16))
        down_sum = down_sum + down_round.astype(jnp.float32)
        up_sum = up_sum + up_round.astype(jnp.float32)
    adapter_output_rows = jnp.concatenate(delta_list, axis=0)
    adapter_gradient_input = jnp.concatenate(input_collection, axis=0)
    mixed_out = (base + adapter_output_rows.astype(jnp.float32)).astype(jnp.bfloat16)
    token_input_gradient = (frozen_gradient + adapter_gradient_input.astype(jnp.float32)).astype(jnp.bfloat16)
    return (mixed_out, token_input_gradient, down_sum.astype(jnp.bfloat16), up_sum.astype(jnp.bfloat16))
```

```python
import jax
import jax.numpy as jnp
from jax import lax
from jax.sharding import PartitionSpec as P

ADAPTER_SCALE = 0.5
CHUNKS = 2
SPLIT = 128


def exchange(pieces, axes):
    return lax.all_to_all(pieces, axes, split_axis=0, concat_axis=0, tiled=True)


def column_blocks(matrix, blocks):
    width = matrix.shape[1] // blocks
    return jnp.stack([matrix[:, i * width : (i + 1) * width] for i in range(blocks)])


def shift(array, axis, step):
    size = lax.axis_size(axis)
    return lax.ppermute(array, axis, [(i, (i + step) % size) for i in range(size)])


def tensor_sum(partial):
    size = lax.axis_size("tensor")
    total = partial
    bit = 1
    while bit < size:
        other = lax.ppermute(total, "tensor", [(i, i ^ bit) for i in range(size)])
        total = (total.astype(jnp.float32) + other.astype(jnp.float32)).astype(jnp.bfloat16)
        bit *= 2
    return total


def dot(a, b, ca, cb):
    return lax.dot_general(a, b, (((ca,), (cb,)), ((), ())), preferred_element_type=jnp.float32)


class Columns:
    def __init__(self, first, adapters, rank, parts):
        width = adapters * rank
        column = jnp.arange(width, dtype=jnp.int32)
        piece = rank // parts
        self.slot = first + (column % (adapters * piece)) // piece
        self.rank = (column // (adapters * piece)) * piece + column % piece
        self.select = (jnp.arange(rank, dtype=jnp.int32)[:, None] == self.rank[None, :]).astype(
            jnp.bfloat16
        )

    def spread(self, compact, slots):
        mine = slots[:, None] == self.slot[None, :]
        return jnp.where(mine, dot(compact, self.select, 1, 0), 0.0).astype(jnp.bfloat16)

    def gather(self, full, slots):
        mine = slots[:, None] == self.slot[None, :]
        return dot(jnp.where(mine, full, 0.0).astype(jnp.bfloat16), self.select, 1, 1)


def shards(
    tokens,
    frozen_value_weight,
    adapter_down_weight,
    adapter_up_weight,
    cotangent,
    language_pair_index,
    language_pair_counts,
    adapter_owner_table,
):
    sides = lax.axis_size("adapter")
    shares = lax.axis_size("tensor")
    planes = lax.axis_size("dp")
    side = lax.axis_index("adapter")
    share = lax.axis_index("tensor")
    plane = lax.axis_index("dp")
    rows, width = tokens.shape
    stored, rank, _ = adapter_down_weight.shape
    values = cotangent.shape[1]
    value_width = values // shares
    own = shares * stored
    total = sides * own
    piece = rank // planes

    down_flat = adapter_down_weight.reshape(stored * rank, shares * width)
    up_flat = adapter_up_weight.reshape(stored * rank, values)

    def to_all(blocks):
        return jnp.broadcast_to(blocks[None], (sides,) + blocks.shape).reshape(
            (sides * shares,) + blocks.shape[1:]
        )

    ups = exchange(to_all(column_blocks(up_flat, shares)), ("adapter", "tensor"))
    ups = ups.reshape(total * rank, value_width)
    quarter = lax.dynamic_slice_in_dim(adapter_down_weight, plane * piece, piece, 1)
    quarter = column_blocks(quarter.reshape(stored * piece, shares * width), shares)
    quarters = exchange(to_all(quarter), ("adapter", "tensor")).reshape(
        sides, own * piece, width
    )
    own_down = exchange(column_blocks(down_flat, shares), "tensor").reshape(own * rank, width)
    other_downs = [
        lax.all_gather(
            lax.dynamic_index_in_dim(quarters, (side - j) % sides, 0, keepdims=False),
            "dp",
            axis=0,
            tiled=True,
        )
        for j in range(1, sides)
    ]

    pairs = jnp.arange(adapter_owner_table.shape[0], dtype=jnp.int32)
    matches = language_pair_index[:, None] == pairs[None, :]
    slots = jnp.sum(jnp.where(matches, adapter_owner_table[None, :], 0), axis=1)
    row_counts = jnp.sum(jnp.where(matches, language_pair_counts[0][None, :], 0), axis=1)
    row_weight = 1.0 / row_counts.astype(jnp.float32)
    scaled = (cotangent.astype(jnp.float32) * row_weight[:, None]).astype(jnp.bfloat16)
    scaled_part = lax.dynamic_slice_in_dim(scaled, share * value_width, value_width, 1)

    every = Columns(0, total, rank, 1)
    mine = Columns(side * own, own, rank, 1)
    mine_parts = Columns(side * own, own, rank, planes)
    others = [Columns(((side - j) % sides) * own, own, rank, planes) for j in range(1, sides)]

    base_term = dot(tokens, frozen_value_weight, 1, 0).astype(jnp.bfloat16)
    base_share = lax.psum_scatter(base_term, "tensor", scatter_dimension=1, tiled=True)

    back_part = every.gather(ADAPTER_SCALE * dot(scaled_part, ups, 1, 1), slots)
    back = tensor_sum(back_part.astype(jnp.bfloat16))

    tag = jnp.stack([slots // SPLIT, slots % SPLIT], axis=1).astype(jnp.bfloat16)
    message = jnp.concatenate([back, tag], axis=1)
    messages = [message] + [shift(message, "adapter", j) for j in range(1, sides)]
    spread_back = []
    for got in messages:
        numbers = got[:, rank:].astype(jnp.int32)
        spread_back.append(
            mine_parts.spread(got[:, :rank], numbers[:, 0] * SPLIT + numbers[:, 1])
        )

    chunk = width // CHUNKS
    down_chunks = []
    for c in range(CHUNKS):
        block = tokens[:, c * chunk : (c + 1) * chunk]
        blocks = [block] + [shift(block, "adapter", j) for j in range(1, sides)]
        part = sum(dot(b, g, 0, 0) for b, g in zip(spread_back, blocks))
        part = part.astype(jnp.bfloat16).reshape(planes * shares, stored * piece, chunk)
        parts = exchange(part, ("dp", "tensor"))
        parts = parts.reshape(planes, shares, stored * piece, chunk)
        down_chunks.append(jnp.sum(parts.astype(jnp.float32), axis=0).astype(jnp.bfloat16))
    grad_down = jnp.concatenate(
        [down_chunks[c][s] for s in range(shares) for c in range(CHUNKS)], axis=1
    ).reshape(stored, piece, shares * width)

    input_gradient = dot(scaled, frozen_value_weight, 1, 1)
    input_gradient += dot(mine.spread(back, slots), own_down, 1, 0)
    low_part = mine.gather(dot(tokens, own_down, 1, 1), slots)
    for columns, other_down in zip(others, other_downs):
        input_gradient += dot(columns.spread(back, slots), other_down, 1, 0)
        low_part += columns.gather(dot(tokens, other_down, 1, 1), slots)
    low = tensor_sum(low_part.astype(jnp.bfloat16))

    spread_low = every.spread(low, slots)
    delta = ADAPTER_SCALE * dot(spread_low, ups, 1, 0)
    mixed_out = (base_share.astype(jnp.float32) + delta).astype(jnp.bfloat16)
    up_part = (ADAPTER_SCALE * dot(spread_low, scaled_part, 0, 0)).astype(jnp.bfloat16)
    up_part = up_part.reshape(sides, shares, stored, planes, piece, value_width)
    up_part = up_part.transpose(3, 0, 1, 2, 4, 5).reshape(
        planes * sides * shares, stored * piece, value_width
    )
    up_parts = exchange(up_part, ("dp", "adapter", "tensor"))
    up_parts = up_parts.reshape(planes * sides, shares, stored * piece, value_width)
    up_sum = jnp.sum(up_parts.astype(jnp.float32), axis=0).astype(jnp.bfloat16)
    grad_up = jnp.concatenate([up_sum[s] for s in range(shares)], axis=1).reshape(
        stored, piece, values
    )
    return mixed_out, input_gradient.astype(jnp.bfloat16), grad_down, grad_up


def solution(mesh):
    return jax.shard_map(
        shards,
        mesh=mesh,
        in_specs=(
            P(("dp", "adapter"), "tensor"),
            P("tensor", None),
            P(("adapter", "tensor"), None, None),
            P(("adapter", "tensor"), None, None),
            P(("dp", "adapter"), None),
            P(("dp", "adapter")),
            P(("dp", "adapter"), None),
            P(),
        ),
        out_specs=(
            P(("dp", "adapter"), "tensor"),
            P(("dp", "adapter"), "tensor"),
            P(("adapter", "tensor"), "dp", None),
            P(("adapter", "tensor"), "dp", None),
        ),
        check_vma=False,
    )
```

```python
import jax
import jax.numpy as jnp
from jax import lax
from jax.sharding import PartitionSpec as P

ADAPTER_SCALE = 0.5
CHUNKS = 2
SPLIT = 128


def exchange(pieces, axes):
    return lax.all_to_all(pieces, axes, split_axis=0, concat_axis=0, tiled=True)


def column_blocks(matrix, blocks):
    width = matrix.shape[1] // blocks
    return jnp.stack([matrix[:, i * width : (i + 1) * width] for i in range(blocks)])


def shift(array, axis, step):
    size = lax.axis_size(axis)
    return lax.ppermute(array, axis, [(i, (i + step) % size) for i in range(size)])


def tensor_sum(partial):
    size = lax.axis_size("tensor")
    total = partial
    bit = 1
    while bit < size:
        other = lax.ppermute(total, "tensor", [(i, i ^ bit) for i in range(size)])
        total = (total.astype(jnp.float32) + other.astype(jnp.float32)).astype(jnp.bfloat16)
        bit *= 2
    return total


def dot(a, b, ca, cb):
    return lax.dot_general(a, b, (((ca,), (cb,)), ((), ())), preferred_element_type=jnp.float32)


class Columns:
    def __init__(self, first, adapters, rank, parts):
        width = adapters * rank
        column = jnp.arange(width, dtype=jnp.int32)
        piece = rank // parts
        self.slot = first + (column % (adapters * piece)) // piece
        self.rank = (column // (adapters * piece)) * piece + column % piece
        self.select = (jnp.arange(rank, dtype=jnp.int32)[:, None] == self.rank[None, :]).astype(
            jnp.bfloat16
        )

    def spread(self, compact, slots):
        mine = slots[:, None] == self.slot[None, :]
        return jnp.where(mine, dot(compact, self.select, 1, 0), 0.0).astype(jnp.bfloat16)

    def gather(self, full, slots):
        mine = slots[:, None] == self.slot[None, :]
        return dot(jnp.where(mine, full, 0.0).astype(jnp.bfloat16), self.select, 1, 1).astype(
            jnp.bfloat16
        )


def after(value, *earlier):
    return lax.optimization_barrier((value,) + earlier)[0]


def scatter_columns(term):
    size = lax.axis_size("tensor")
    share = lax.axis_index("tensor")
    width = term.shape[1] // size
    blocks = [
        lax.dynamic_slice_in_dim(term, (share ^ i) * width, width, 1) for i in range(size)
    ]
    bit = 1
    while bit < size:
        pairs = [(i, i ^ bit) for i in range(size)]
        kept = [i for i in range(size) if i % (2 * bit) == 0]
        send = jnp.concatenate([blocks[i ^ bit] for i in kept], axis=1)
        got = lax.ppermute(send, "tensor", pairs)
        for n, i in enumerate(kept):
            blocks[i] = (
                blocks[i].astype(jnp.float32)
                + got[:, n * width : (n + 1) * width].astype(jnp.float32)
            ).astype(jnp.bfloat16)
        bit *= 2
    return blocks[0]


def shards(
    tokens,
    frozen_value_weight,
    adapter_down_weight,
    adapter_up_weight,
    cotangent,
    language_pair_index,
    language_pair_counts,
    adapter_owner_table,
):
    sides = lax.axis_size("adapter")
    shares = lax.axis_size("tensor")
    planes = lax.axis_size("dp")
    side = lax.axis_index("adapter")
    share = lax.axis_index("tensor")
    rows, width = tokens.shape
    stored, rank, _ = adapter_down_weight.shape
    values = cotangent.shape[1]
    value_width = values // shares
    own = shares * stored
    total = sides * own
    piece = rank // planes
    steps = range(1, sides)

    pairs = jnp.arange(adapter_owner_table.shape[0], dtype=jnp.int32)
    matches = language_pair_index[:, None] == pairs[None, :]
    slots = jnp.sum(jnp.where(matches, adapter_owner_table[None, :], 0), axis=1)
    row_counts = jnp.sum(jnp.where(matches, language_pair_counts[0][None, :], 0), axis=1)
    row_weight = 1.0 / row_counts.astype(jnp.float32)
    scaled = (cotangent.astype(jnp.float32) * row_weight[:, None]).astype(jnp.bfloat16)
    scaled_part = lax.dynamic_slice_in_dim(scaled, share * value_width, value_width, 1)

    tag_rows = -(-rows // value_width)
    tags = jnp.pad(slots, (0, tag_rows * value_width - rows)).reshape(tag_rows, value_width)
    tags = jnp.concatenate([tags // SPLIT, tags % SPLIT]).astype(jnp.bfloat16)
    tags = jnp.pad(tags, ((0, -2 * tag_rows % 16), (0, 0)))
    message = jnp.concatenate([scaled_part, tags])
    scaled_of, slots_of = [scaled_part], [slots]
    for j in steps:
        got = shift(message, "adapter", j)
        scaled_of.append(got[:rows])
        numbers = got[rows : rows + 2 * tag_rows].astype(jnp.int32)
        numbers = numbers[:tag_rows] * SPLIT + numbers[tag_rows:]
        slots_of.append(numbers.reshape(-1)[:rows])

    up_blocks = column_blocks(adapter_up_weight.reshape(stored * rank, values), shares)
    up_blocks = jnp.broadcast_to(up_blocks[None], (sides,) + up_blocks.shape)
    ups = exchange(
        up_blocks.reshape(sides * shares, stored * rank, value_width), ("adapter", "tensor")
    ).reshape(total * rank, value_width)
    own_ups = lax.dynamic_slice_in_dim(ups, side * own * rank, own * rank, 0)
    own_down = exchange(
        column_blocks(adapter_down_weight.reshape(stored * rank, shares * width), shares), "tensor"
    ).reshape(own * rank, width)

    chunk = width // CHUNKS
    token_chunks = []
    for c in range(CHUNKS):
        block = tokens[:, c * chunk : (c + 1) * chunk]
        token_chunks.append([block] + [shift(block, "adapter", j) for j in steps])
    crossed = token_chunks[-1][1:]
    other_downs = [shift(after(own_down, *crossed), "adapter", j) for j in steps]

    every = Columns(0, total, rank, 1)
    mine = Columns(side * own, own, rank, 1)
    mine_parts = Columns(side * own, own, rank, planes)
    others = [Columns(((side - j) % sides) * own, own, rank, 1) for j in steps]

    def over_tensor(parts):
        joined = tensor_sum(jnp.concatenate(parts, axis=1))
        return [joined[:, i * rank : (i + 1) * rank] for i in range(sides)]

    base_term = dot(tokens, frozen_value_weight, 1, 0).astype(jnp.bfloat16)
    base_share = scatter_columns(base_term)

    back_of = over_tensor(
        [
            mine.gather(ADAPTER_SCALE * dot(part, own_ups, 1, 1), numbers)
            for part, numbers in zip(scaled_of, slots_of)
        ]
    )
    spread_back = [mine_parts.spread(b, n) for b, n in zip(back_of, slots_of)]

    low_full = [0.0] * sides
    parts_down = []
    for c in range(CHUNKS):
        part = sum(dot(b, g, 0, 0) for b, g in zip(spread_back, token_chunks[c]))
        parts_down.append(part.astype(jnp.bfloat16))
        weights = own_down[:, c * chunk : (c + 1) * chunk]
        for i in range(sides):
            low_full[i] += dot(token_chunks[c][i], weights, 1, 1)
    low_of = over_tensor([mine.gather(f, n) for f, n in zip(low_full, slots_of)])
    up_part = ADAPTER_SCALE * sum(
        dot(mine_parts.spread(v, n), part, 0, 0)
        for v, n, part in zip(low_of, slots_of, scaled_of)
    )
    parts_down[-1] = jnp.concatenate([parts_down[-1], up_part.astype(jnp.bfloat16)], axis=1)

    sums = []
    for part in parts_down:
        columns = part.shape[1]
        got = exchange(part.reshape(planes * shares, stored * piece, columns), ("dp", "tensor"))
        got = got.reshape(planes, shares, stored * piece, columns)
        sums.append(jnp.sum(got.astype(jnp.float32), axis=0).astype(jnp.bfloat16))
    grad_down = jnp.concatenate(
        [sums[c][s][:, :chunk] for s in range(shares) for c in range(CHUNKS)], axis=1
    ).reshape(stored, piece, shares * width)
    grad_up = jnp.concatenate([sums[-1][s][:, chunk:] for s in range(shares)], axis=1).reshape(
        stored, piece, values
    )

    low, back = low_of[0], back_of[0]
    for j in steps:
        reply = shift(jnp.concatenate([low_of[j], back_of[j]], axis=1), "adapter", -j)
        low = low + reply[:, :rank]
        back = back + reply[:, rank:]
    delta = ADAPTER_SCALE * dot(every.spread(low, slots), ups, 1, 0)
    mixed_out = (base_share.astype(jnp.float32) + delta).astype(jnp.bfloat16)

    input_gradient = dot(scaled, frozen_value_weight, 1, 1)
    input_gradient += dot(mine.spread(back, slots), own_down, 1, 0)
    for columns, other_down in zip(others, other_downs):
        input_gradient += dot(columns.spread(back, slots), other_down, 1, 0)
    return mixed_out, input_gradient.astype(jnp.bfloat16), grad_down, grad_up


def solution(mesh):
    return jax.shard_map(
        shards,
        mesh=mesh,
        in_specs=(
            P(("dp", "adapter"), "tensor"),
            P("tensor", None),
            P(("adapter", "tensor"), None, None),
            P(("adapter", "tensor"), None, None),
            P(("dp", "adapter"), None),
            P(("dp", "adapter")),
            P(("dp", "adapter"), None),
            P(),
        ),
        out_specs=(
            P(("dp", "adapter"), "tensor"),
            P(("dp", "adapter"), "tensor"),
            P(("adapter", "tensor"), "dp", None),
            P(("adapter", "tensor"), "dp", None),
        ),
        check_vma=False,
    )
```

```python
import functools

import jax
import jax.numpy as jnp
from jax import lax
from jax.experimental import pallas as pl
from jax.experimental.pallas import tpu as pltpu
from jax.sharding import PartitionSpec as P

ADAPTER_SCALE = 0.5
PIECES = (2, 4, 4)
SPLIT = 128
LANES = 128
VMEM = 56 * 1024 * 1024


def exchange(pieces, axes):
    return lax.all_to_all(pieces, axes, split_axis=0, concat_axis=0, tiled=True)


def shift(array, axis, step):
    size = lax.axis_size(axis)
    return lax.ppermute(array, axis, [(i, (i + step) % size) for i in range(size)])


def swap(array, axis, bit):
    return lax.ppermute(array, axis, [(i, i ^ bit) for i in range(lax.axis_size(axis))])


def after(value, *earlier):
    return lax.optimization_barrier((value,) + earlier)[0]


def add(a, b):
    return (a.astype(jnp.float32) + b.astype(jnp.float32)).astype(jnp.bfloat16)


def bits_below(size):
    return [1 << i for i in range(size.bit_length() - 1)]


def tensor_sum(total):
    for bit in bits_below(lax.axis_size("tensor")):
        total = add(total, swap(total, "tensor", bit))
    return total


def scatter_columns(term):
    size = lax.axis_size("tensor")
    share = lax.axis_index("tensor")
    width = term.shape[1] // size
    blocks = [
        lax.dynamic_slice_in_dim(term, (share ^ i) * width, width, 1) for i in range(size)
    ]
    for bit in bits_below(size):
        kept = [i for i in range(size) if i % (2 * bit) == 0]
        got = swap(jnp.concatenate([blocks[i ^ bit] for i in kept], axis=1), "tensor", bit)
        for n, i in enumerate(kept):
            blocks[i] = add(blocks[i], got[:, n * width : (n + 1) * width])
    return blocks[0]


def dot(a, b, ca, cb):
    return lax.dot_general(a, b, (((ca,), (cb,)), ((), ())), preferred_element_type=jnp.float32)


def call(body, grid, in_specs, out_spec, out_shape, operands, flops, scratch=()):
    moved = sum(x.size * x.dtype.itemsize for x in operands)
    return pl.pallas_call(
        body,
        grid=grid,
        in_specs=in_specs,
        out_specs=out_spec,
        out_shape=out_shape,
        scratch_shapes=list(scratch),
        compiler_params=pltpu.CompilerParams(vmem_limit_bytes=VMEM),
        cost_estimate=pl.CostEstimate(flops=flops, bytes_accessed=moved, transcendentals=0),
    )(*operands)


def whole(array):
    return pl.BlockSpec(array.shape, lambda i: (0,) * array.ndim)


def fold_body(count, rank, scale, *refs):
    lines, weight, column_slots, slots = refs[:count], refs[count], refs[count + 1], refs[count + 2]
    out = refs[-1]
    step = max(rank, LANES)
    results = []
    for n in range(count):
        full = dot(lines[n][...], weight[...], 1, 1)
        full = jnp.where(slots[:, n : n + 1] == column_slots[...], full, 0.0)
        total = full[:, :step]
        for i in range(step, full.shape[1], step):
            total += full[:, i : i + step]
        results.append(sum(total[:, i : i + rank] for i in range(0, step, rank)))
    result = scale * jnp.concatenate(results, axis=1)
    if len(refs) == count + 5:
        result += refs[count + 3][...]
    out[...] = result.astype(out.dtype)


def fold_product(lines, weight, block, column_slots, slots, rank, scale, before, dtype):
    count = len(lines)
    rows = slots.shape[0]
    tile = rows // 2
    offset, depth = block
    specs = [
        pl.BlockSpec((tile, depth), functools.partial(lambda o, i: (i, o), 0))
        if line.shape[1] == depth
        else pl.BlockSpec((tile, depth), lambda i: (i, offset))
        for line in lines
    ]
    specs.append(pl.BlockSpec((weight.shape[0], depth), lambda i: (0, offset)))
    specs.append(whole(column_slots))
    specs.append(pl.BlockSpec((tile, count), lambda i: (i, 0)))
    operands = list(lines) + [weight, column_slots, slots]
    out_spec = pl.BlockSpec((tile, count * rank), lambda i: (i, 0))
    if before is not None:
        specs.append(out_spec)
        operands.append(before)
    return call(
        functools.partial(fold_body, count, rank, scale),
        (2,),
        specs,
        out_spec,
        jax.ShapeDtypeStruct((rows, count * rank), dtype),
        operands,
        2 * count * rows * weight.shape[0] * depth,
    )


def weight_body(count, rank, scale, *refs):
    compact, row_slots, column_slots, select = refs[:4]
    lines, out, spread = refs[4 : 4 + count], refs[-2], refs[-1]

    @pl.when(pl.program_id(0) == 0)
    def _():
        for n in range(count):
            wide = dot(select[...], compact[:, n * rank : (n + 1) * rank], 1, 1)
            mine = column_slots[...] == row_slots[n : n + 1, :]
            spread[n] = jnp.where(mine, wide, 0.0).astype(jnp.bfloat16)

    total = dot(spread[0], lines[0][...], 1, 0)
    for n in range(1, count):
        total += dot(spread[n], lines[n][...], 1, 0)
    out[...] = (scale * total).astype(out.dtype)


def weight_product(compact, row_slots, column_slots, select, lines, block, scale):
    count = len(lines)
    rows = row_slots.shape[1]
    columns, rank = select.shape
    offset, width = block
    tile = min(width, 512)
    per = width // tile
    specs = [whole(x) for x in (compact, row_slots, column_slots, select)]
    for line in lines:
        skip = 0 if line.shape[1] == width else offset * per
        specs.append(pl.BlockSpec((rows, tile), functools.partial(lambda s, i: (0, s + i), skip)))
    return call(
        functools.partial(weight_body, count, rank, scale),
        (per,),
        specs,
        pl.BlockSpec((columns, tile), lambda i: (0, i)),
        jax.ShapeDtypeStruct((columns, width), jnp.bfloat16),
        [compact, row_slots, column_slots, select] + list(lines),
        2 * count * rows * columns * width,
        [pltpu.VMEM((count, columns, rows), jnp.bfloat16)],
    )


def input_body(count, *refs):
    scaled, frozen, compact, slots, column_slots, select = refs[:6]
    downs, out, spread = refs[6 : 6 + count], refs[-2], refs[-1]

    @pl.when(pl.program_id(0) == 0)
    def _():
        for n in range(count):
            wide = dot(compact[...], select[n], 1, 0)
            mine = slots[...] == column_slots[n : n + 1, :]
            spread[n] = jnp.where(mine, wide, 0.0).astype(jnp.bfloat16)

    total = dot(scaled[...], frozen[...], 1, 1)
    for n in range(count):
        total += dot(spread[n], downs[n][...], 1, 0)
    out[...] = total.astype(out.dtype)


def input_product(scaled, frozen, compact, slots, column_slots, select, downs):
    count = len(downs)
    rows, values = scaled.shape
    columns, width = downs[0].shape
    tile = max(LANES, 1024 // count)
    specs = [whole(scaled), pl.BlockSpec((tile, values), lambda i: (i, 0))]
    specs += [whole(x) for x in (compact, slots, column_slots, select)]
    specs += [pl.BlockSpec((columns, tile), lambda i: (0, i))] * count
    return call(
        functools.partial(input_body, count),
        (width // tile,),
        specs,
        pl.BlockSpec((rows, tile), lambda i: (0, i)),
        jax.ShapeDtypeStruct((rows, width), jnp.bfloat16),
        [scaled, frozen, compact, slots, column_slots, select] + list(downs),
        2 * rows * width * (values + count * columns),
        [pltpu.VMEM((count, rows, columns), jnp.bfloat16)],
    )


def output_body(base, compact, slots, column_slots, select, ups, out):
    wide = dot(compact[...], select[...], 1, 0)
    spread = jnp.where(slots[...] == column_slots[...], wide, 0.0).astype(jnp.bfloat16)
    delta = ADAPTER_SCALE * dot(spread, ups[...], 1, 0)
    out[...] = (base[...].astype(jnp.float32) + delta).astype(out.dtype)


def output_product(base, compact, slots, column_slots, select, ups):
    rows, width = base.shape
    tile = rows // 2 if ups.shape[0] <= 2048 else 64
    line = lambda i: (i, 0)
    specs = [pl.BlockSpec((tile, x.shape[1]), line) for x in (base, compact, slots)]
    specs += [whole(x) for x in (column_slots, select, ups)]
    return call(
        output_body,
        (rows // tile,),
        specs,
        pl.BlockSpec((tile, width), line),
        jax.ShapeDtypeStruct((rows, width), jnp.bfloat16),
        [base, compact, slots, column_slots, select, ups],
        2 * rows * width * ups.shape[0],
    )


def choose(ranks, rank):
    return (jnp.arange(rank, dtype=jnp.int32)[:, None] == ranks[None, :]).astype(jnp.bfloat16)


def shards(
    tokens,
    frozen_value_weight,
    adapter_down_weight,
    adapter_up_weight,
    cotangent,
    language_pair_index,
    language_pair_counts,
    adapter_owner_table,
):
    sides = lax.axis_size("adapter")
    shares = lax.axis_size("tensor")
    planes = lax.axis_size("dp")
    side = lax.axis_index("adapter")
    share = lax.axis_index("tensor")
    plane = lax.axis_index("dp")
    rows, width = tokens.shape
    stored, rank, _ = adapter_down_weight.shape
    values = cotangent.shape[1]
    value_width = values // shares
    own = shares * stored
    total = sides * own
    piece = rank // planes
    lot = stored * piece
    steps = range(1, sides)

    quarter = lax.dynamic_slice_in_dim(adapter_down_weight, plane * piece, piece, 1)
    quarter = quarter.reshape(lot, shares * width)
    up_flat = adapter_up_weight.reshape(stored * rank, values)
    parcel = jnp.stack(
        [
            jnp.concatenate(
                [quarter[:, s * width : (s + 1) * width]]
                + [
                    up_flat[g * lot : (g + 1) * lot, s * value_width : (s + 1) * value_width]
                    for g in range(planes)
                ],
                axis=1,
            )
            for s in range(shares)
        ]
    )
    parcel = jnp.broadcast_to(parcel[None], (sides,) + parcel.shape)
    got = exchange(parcel.reshape((sides * shares,) + parcel.shape[2:]), ("adapter", "tensor"))
    ups = jnp.stack(
        [
            got[:, :, width + g * value_width : width + (g + 1) * value_width]
            for g in range(planes)
        ],
        axis=1,
    ).reshape(total * rank, value_width)
    own_ups = lax.dynamic_slice_in_dim(ups, side * own * rank, own * rank, 0)
    other_downs = []
    for j in steps:
        block = lax.dynamic_slice(
            got, (((side - j) % sides) * shares, 0, 0), (shares, lot, width)
        ).reshape(own * piece, width)
        order = [0]
        for bit in reversed(bits_below(planes)):
            block = jnp.concatenate([block, swap(block, "dp", bit)])
            order += [o ^ bit for o in order]
        other_downs.append(block)

    pairs = jnp.arange(adapter_owner_table.shape[0], dtype=jnp.int32)
    matches = language_pair_index[:, None] == pairs[None, :]
    slots = jnp.sum(jnp.where(matches, adapter_owner_table[None, :], 0), axis=1)
    row_counts = jnp.sum(jnp.where(matches, language_pair_counts[0][None, :], 0), axis=1)
    row_weight = 1.0 / row_counts.astype(jnp.float32)
    scaled = (cotangent.astype(jnp.float32) * row_weight[:, None]).astype(jnp.bfloat16)
    scaled_part = lax.dynamic_slice_in_dim(scaled, share * value_width, value_width, 1)

    tag_rows = -(-rows // value_width)
    tags = jnp.pad(slots, (0, tag_rows * value_width - rows)).reshape(tag_rows, value_width)
    tags = jnp.concatenate([tags // SPLIT, tags % SPLIT]).astype(jnp.bfloat16)
    tags = jnp.pad(tags, ((0, -2 * tag_rows % 16), (0, 0)))
    message = jnp.concatenate([scaled_part, tags])
    scaled_of, slots_of = [scaled_part], [slots]
    for j in steps:
        answer = shift(message, "adapter", j)
        scaled_of.append(answer[:rows])
        numbers = answer[rows : rows + 2 * tag_rows].astype(jnp.int32)
        numbers = numbers[:tag_rows] * SPLIT + numbers[tag_rows:]
        slots_of.append(numbers.reshape(-1)[:rows])
    row_slots = jnp.stack(slots_of)
    slot_columns = row_slots.T

    pieces, position = [], 0
    for part in PIECES:
        piece_width = width // part
        others = tokens[:, position : position + piece_width]
        pieces.append(
            (
                (position // piece_width, piece_width),
                [tokens] + [shift(others, "adapter", j) for j in steps],
            )
        )
        position += piece_width

    base_term = dot(tokens, frozen_value_weight, 1, 0).astype(jnp.bfloat16)
    base_share = scatter_columns(base_term)

    column = jnp.arange(own * rank, dtype=jnp.int32)
    sent_slots = (side * shares + (share ^ (column // (stored * rank)))) * stored
    sent_slots += (column // rank) % stored
    part_local = (column % (own * piece)) // piece
    part_ranks = (column // (own * piece)) * piece + column % piece
    part_slots = side * own + part_local
    natural_slots = side * own + column // rank
    part_select = choose(part_ranks, rank).T

    back_part = fold_product(
        scaled_of,
        own_ups,
        (0, value_width),
        natural_slots[None, :],
        slot_columns,
        rank,
        ADAPTER_SCALE,
        None,
        jnp.bfloat16,
    )
    back_all = tensor_sum(back_part)

    down_flat = after(adapter_down_weight.reshape(stored * rank, shares * width), back_all)
    sent = [
        lax.dynamic_slice_in_dim(down_flat, (share ^ k) * width, width, 1) for k in range(shares)
    ]
    own_down = jnp.concatenate(
        [sent[0]] + [swap(sent[k], "tensor", k) for k in range(1, shares)]
    )

    low_part = None
    parts_down = []
    for n, (block, lines) in enumerate(pieces):
        parts_down.append(
            weight_product(
                back_all, row_slots, part_slots[:, None], part_select, lines, block, 1.0
            )
        )
        last = n == len(pieces) - 1
        low_part = fold_product(
            lines,
            own_down,
            block,
            sent_slots[None, :],
            slot_columns,
            rank,
            1.0,
            low_part,
            jnp.bfloat16 if last else jnp.float32,
        )
    low_all = tensor_sum(low_part)
    up_part = weight_product(
        low_all,
        row_slots,
        part_slots[:, None],
        part_select,
        scaled_of,
        (0, value_width),
        ADAPTER_SCALE,
    )
    last_width = parts_down[-1].shape[1]
    parts_down[-1] = jnp.concatenate([parts_down[-1], up_part], axis=1)

    sums = []
    for part in parts_down:
        columns = part.shape[1]
        arrived = exchange(part.reshape(planes * shares, lot, columns), ("dp", "tensor"))
        arrived = arrived.reshape(planes, shares, lot, columns)
        sums.append(jnp.sum(arrived.astype(jnp.float32), axis=0).astype(jnp.bfloat16))
    grad_down = jnp.concatenate(
        [
            sums[n][s][:, : pieces[n][0][1]]
            for s in range(shares)
            for n in range(len(pieces))
        ],
        axis=1,
    ).reshape(stored, piece, shares * width)
    grad_up = jnp.concatenate(
        [sums[-1][s][:, last_width:] for s in range(shares)], axis=1
    ).reshape(stored, piece, values)

    low, back = low_all[:, :rank], back_all[:, :rank]
    for j in steps:
        here = slice(j * rank, (j + 1) * rank)
        reply = jnp.concatenate([low_all[:, here], back_all[:, here]], axis=1)
        reply = shift(reply, "adapter", -j)
        low = low + reply[:, :rank]
        back = back + reply[:, rank:]

    every = jnp.arange(total * rank, dtype=jnp.int32)
    mixed_out = output_product(
        base_share, low, slots[:, None], (every // rank)[None, :], choose(every % rank, rank), ups
    )

    base_of = jnp.array(order, jnp.int32)[column // (own * piece)]
    other_ranks = (plane ^ base_of) * piece + column % piece
    input_gradient = input_product(
        scaled,
        frozen_value_weight,
        back,
        slots[:, None],
        jnp.stack(
            [sent_slots] + [((side - j) % sides) * own + part_local for j in steps]
        ),
        jnp.stack([choose(column % rank, rank)] + [choose(other_ranks, rank) for _ in steps]),
        [own_down] + other_downs,
    )
    return mixed_out, input_gradient, grad_down, grad_up


def solution(mesh):
    return jax.shard_map(
        shards,
        mesh=mesh,
        in_specs=(
            P(("dp", "adapter"), "tensor"),
            P("tensor", None),
            P(("adapter", "tensor"), None, None),
            P(("adapter", "tensor"), None, None),
            P(("dp", "adapter"), None),
            P(("dp", "adapter")),
            P(("dp", "adapter"), None),
            P(),
        ),
        out_specs=(
            P(("dp", "adapter"), "tensor"),
            P(("dp", "adapter"), "tensor"),
            P(("adapter", "tensor"), "dp", None),
            P(("adapter", "tensor"), "dp", None),
        ),
        check_vma=False,
    )
```

```python
import functools

import jax
import jax.numpy as jnp
from jax import lax
from jax.experimental import pallas as pl
from jax.experimental.pallas import tpu as pltpu
from jax.sharding import Mesh
from jax.sharding import PartitionSpec as P

ADAPTER_SCALE = 0.5
PIECES = (2, 2)
SPLIT = 128
HINT = 1000
LANES = 128
VMEM = 56 * 1024 * 1024


def exchange(pieces, axes):
    return lax.all_to_all(pieces, axes, split_axis=0, concat_axis=0, tiled=True)


def shift(array, axis, step):
    size = lax.axis_size(axis)
    return lax.ppermute(array, axis, [(i, (i + step) % size) for i in range(size)])


def swap(array, axis, bit):
    return lax.ppermute(array, axis, [(i, i ^ bit) for i in range(lax.axis_size(axis))])


def after(value, *earlier):
    return lax.optimization_barrier((value,) + earlier)[0]


def add(a, b):
    return (a.astype(jnp.float32) + b.astype(jnp.float32)).astype(jnp.bfloat16)


def bits_below(size):
    return [1 << i for i in range(size.bit_length() - 1)]


def tensor_sum(total, bits=None):
    for bit in bits_below(lax.axis_size("tensor")) if bits is None else bits:
        total = add(total, swap(total, "tensor", bit))
    return total


def scatter_columns(term):
    size = lax.axis_size("tensor")
    share = lax.axis_index("tensor")
    width = term.shape[1] // size
    blocks = [
        lax.dynamic_slice_in_dim(term, (share ^ i) * width, width, 1) for i in range(size)
    ]
    for bit in bits_below(size):
        kept = [i for i in range(size) if i % (2 * bit) == 0]
        got = swap(jnp.concatenate([blocks[i ^ bit] for i in kept], axis=1), "tensor", bit)
        for n, i in enumerate(kept):
            blocks[i] = add(blocks[i], got[:, n * width : (n + 1) * width])
    return blocks[0]


def dot(a, b, ca, cb):
    return lax.dot_general(a, b, (((ca,), (cb,)), ((), ())), preferred_element_type=jnp.float32)


def call(body, grid, in_specs, out_spec, out_shape, operands, flops, scratch=()):
    moved = sum(x.size * x.dtype.itemsize for x in operands)
    return pl.pallas_call(
        body,
        grid=grid,
        in_specs=in_specs,
        out_specs=out_spec,
        out_shape=out_shape,
        scratch_shapes=list(scratch),
        compiler_params=pltpu.CompilerParams(vmem_limit_bytes=VMEM),
        cost_estimate=pl.CostEstimate(flops=flops // HINT, bytes_accessed=moved // HINT, transcendentals=0),
    )(*operands)


def whole(array):
    return pl.BlockSpec(array.shape, lambda i: (0,) * array.ndim)


def fold_body(count, rank, scale, *refs):
    lines, weight, column_slots, slots = refs[:count], refs[count], refs[count + 1], refs[count + 2]
    out = refs[-1]
    step = max(rank, LANES)
    results = []
    for n in range(count):
        full = dot(lines[n][...], weight[...], 1, 1)
        full = jnp.where(slots[:, n : n + 1] == column_slots[...], full, 0.0)
        total = full[:, :step]
        for i in range(step, full.shape[1], step):
            total += full[:, i : i + step]
        results.append(sum(total[:, i : i + rank] for i in range(0, step, rank)))
    result = scale * jnp.concatenate(results, axis=1)
    if len(refs) == count + 5:
        result += refs[count + 3][...]
    out[...] = result.astype(out.dtype)


def fold_product(lines, weight, block, column_slots, slots, rank, scale, before, dtype):
    count = len(lines)
    rows = slots.shape[0]
    tile = rows // 2
    offset, depth = block
    specs = [
        pl.BlockSpec((tile, depth), functools.partial(lambda o, i: (i, o), 0))
        if line.shape[1] == depth
        else pl.BlockSpec((tile, depth), lambda i: (i, offset))
        for line in lines
    ]
    specs.append(pl.BlockSpec((weight.shape[0], depth), lambda i: (0, offset)))
    specs.append(whole(column_slots))
    specs.append(pl.BlockSpec((tile, count), lambda i: (i, 0)))
    operands = list(lines) + [weight, column_slots, slots]
    out_spec = pl.BlockSpec((tile, count * rank), lambda i: (i, 0))
    if before is not None:
        specs.append(out_spec)
        operands.append(before)
    return call(
        functools.partial(fold_body, count, rank, scale),
        (2,),
        specs,
        out_spec,
        jax.ShapeDtypeStruct((rows, count * rank), dtype),
        operands,
        2 * count * rows * weight.shape[0] * depth,
    )


def weight_body(count, rank, scale, *refs):
    compact, row_slots, column_slots, select = refs[:4]
    lines, out, spread = refs[4 : 4 + count], refs[-2], refs[-1]

    @pl.when(pl.program_id(0) == 0)
    def _():
        for n in range(count):
            wide = dot(select[...], compact[:, n * rank : (n + 1) * rank], 1, 1)
            mine = column_slots[...] == row_slots[n : n + 1, :]
            spread[n] = jnp.where(mine, wide, 0.0).astype(jnp.bfloat16)

    total = dot(spread[0], lines[0][...], 1, 0)
    for n in range(1, count):
        total += dot(spread[n], lines[n][...], 1, 0)
    out[...] = (scale * total).astype(out.dtype)


def weight_product(compact, row_slots, column_slots, select, lines, block, scale):
    count = len(lines)
    rows = row_slots.shape[1]
    columns, rank = select.shape
    offset, width = block
    tile = min(width, 512)
    per = width // tile
    specs = [whole(x) for x in (compact, row_slots, column_slots, select)]
    for line in lines:
        skip = 0 if line.shape[1] == width else offset * per
        specs.append(pl.BlockSpec((rows, tile), functools.partial(lambda s, i: (0, s + i), skip)))
    return call(
        functools.partial(weight_body, count, rank, scale),
        (per,),
        specs,
        pl.BlockSpec((columns, tile), lambda i: (0, i)),
        jax.ShapeDtypeStruct((columns, width), jnp.bfloat16),
        [compact, row_slots, column_slots, select] + list(lines),
        2 * count * rows * columns * width,
        [pltpu.VMEM((count, columns, rows), jnp.bfloat16)],
    )


def input_body(count, *refs):
    scaled, frozen, compact, slots = refs[:4]
    columns, selects, downs = (refs[4 + i * count : 4 + (i + 1) * count] for i in range(3))
    out, spreads = refs[-1 - count], refs[-count:]

    @pl.when(pl.program_id(0) == 0)
    def _():
        for n in range(count):
            wide = dot(compact[...], selects[n][...], 1, 0)
            mine = slots[...] == columns[n][...]
            spreads[n][...] = jnp.where(mine, wide, 0.0).astype(jnp.bfloat16)

    total = dot(scaled[...], frozen[...], 1, 1)
    for n in range(count):
        total += dot(spreads[n][...], downs[n][...], 1, 0)
    out[...] = total.astype(out.dtype)


def input_product(scaled, frozen, compact, slots, columns, selects, downs, tile):
    count = len(downs)
    rows, values = scaled.shape
    width = downs[0].shape[1]
    specs = [whole(scaled), pl.BlockSpec((tile, values), lambda i: (i, 0))]
    specs += [whole(x) for x in [compact, slots] + columns + selects]
    specs += [pl.BlockSpec((x.shape[0], tile), lambda i: (0, i)) for x in downs]
    return call(
        functools.partial(input_body, count),
        (width // tile,),
        specs,
        pl.BlockSpec((rows, tile), lambda i: (0, i)),
        jax.ShapeDtypeStruct((rows, width), jnp.bfloat16),
        [scaled, frozen, compact, slots] + columns + selects + list(downs),
        2 * rows * width * (values + sum(x.shape[0] for x in downs)),
        [pltpu.VMEM((rows, x.shape[0]), jnp.bfloat16) for x in downs],
    )


def output_body(count, *refs):
    compact, slots, column_slots, select, ups = refs[count : count + 5]
    out = refs[-1]
    wide = dot(compact[...], select[...], 1, 0)
    spread = jnp.where(slots[...] == column_slots[...], wide, 0.0).astype(jnp.bfloat16)
    result = ADAPTER_SCALE * dot(spread, ups[...], 1, 0)
    for addend in refs[:count]:
        result += addend[...].astype(jnp.float32)
    out[...] = result.astype(out.dtype)


def output_product(addends, compact, slots, column_slots, select, ups):
    rows, width = compact.shape[0], ups.shape[1]
    tile = rows // 2
    line = lambda i: (i, 0)
    operands = list(addends) + [compact, slots]
    specs = [pl.BlockSpec((tile, x.shape[1]), line) for x in operands]
    operands += [column_slots, select, ups]
    specs += [whole(x) for x in operands[-3:]]
    return call(
        functools.partial(output_body, len(addends)),
        (rows // tile,),
        specs,
        pl.BlockSpec((tile, width), line),
        jax.ShapeDtypeStruct((rows, width), jnp.bfloat16),
        operands,
        2 * rows * width * ups.shape[0],
    )


def total_body(planes, shares, width, last_width, value_width, *refs):
    out_down, out_up = refs[-2:]
    position = 0
    for ref in refs[:-2]:
        last = ref is refs[-3]
        columns = last_width if last else ref.shape[2]
        for share in range(shares):
            total = sum(ref[q * shares + share].astype(jnp.float32) for q in range(planes))
            start = share * width + position
            out_down[:, start : start + columns] = total[:, :columns].astype(jnp.bfloat16)
            if last:
                start = share * value_width
                out_up[:, start : start + value_width] = total[:, columns:].astype(jnp.bfloat16)
        position += columns


def total_product(arrived, planes, shares, width, last_width, value_width):
    lot = arrived[0].shape[1]
    shapes = [
        jax.ShapeDtypeStruct((lot, shares * columns), jnp.bfloat16)
        for columns in (width, value_width)
    ]
    return call(
        functools.partial(total_body, planes, shares, width, last_width, value_width),
        (1,),
        [whole(x) for x in arrived],
        [whole(x) for x in shapes],
        shapes,
        arrived,
        1000,
    )


def choose(ranks, rank):
    return (jnp.arange(rank, dtype=jnp.int32)[:, None] == ranks[None, :]).astype(jnp.bfloat16)


def shards(
    tokens,
    frozen_value_weight,
    adapter_down_weight,
    adapter_up_weight,
    cotangent,
    language_pair_index,
    language_pair_counts,
    adapter_owner_table,
):
    sides = lax.axis_size("adapter")
    shares = lax.axis_size("tensor")
    far, near = lax.axis_size("far"), lax.axis_size("near")
    planes = far * near
    side = lax.axis_index("adapter")
    share = lax.axis_index("tensor")
    plane = lax.axis_index(("far", "near"))
    close = lax.axis_index("near")
    rows, width = tokens.shape
    stored, rank, _ = adapter_down_weight.shape
    values = cotangent.shape[1]
    value_width = values // shares
    own = shares * stored
    piece = rank // planes
    lot = stored * piece
    steps = range(1, sides)

    quarter = lax.dynamic_slice_in_dim(adapter_down_weight, plane * piece, piece, 1)
    quarter = quarter.reshape(lot, shares * width)
    parcel = jnp.stack([quarter[:, s * width : (s + 1) * width] for s in range(shares)])
    parcel = jnp.broadcast_to(parcel[None], (sides,) + parcel.shape)
    parcel = parcel.reshape(sides * shares, lot, width)
    got = exchange(parcel, ("adapter", "tensor"))

    quarters = []
    for j in steps:
        block = lax.dynamic_slice(
            got, (((side - j) % sides) * shares, 0, 0), (shares, lot, width)
        ).reshape(own * piece, width)
        quarters.append([block] + [shift(block, "near", i) for i in range(1, near)])
    shared = [block for blocks in quarters for block in blocks]

    pairs = jnp.arange(adapter_owner_table.shape[0], dtype=jnp.int32)
    matches = language_pair_index[:, None] == pairs[None, :]
    slots = jnp.sum(jnp.where(matches, adapter_owner_table[None, :], 0), axis=1)
    row_counts = jnp.sum(jnp.where(matches, language_pair_counts[0][None, :], 0), axis=1)
    row_weight = 1.0 / row_counts.astype(jnp.float32)
    scaled = (cotangent.astype(jnp.float32) * row_weight[:, None]).astype(jnp.bfloat16)
    scaled_part = lax.dynamic_slice_in_dim(scaled, share * value_width, value_width, 1)

    tag_rows = -(-rows // value_width)
    tags = jnp.pad(slots, (0, tag_rows * value_width - rows)).reshape(tag_rows, value_width)
    tags = jnp.concatenate([tags // SPLIT, tags % SPLIT]).astype(jnp.bfloat16)
    tags = jnp.pad(tags, ((0, -2 * tag_rows % 16), (0, 0)))
    message = after(jnp.concatenate([scaled_part, tags]), parcel)
    scaled_of, slots_of = [scaled_part], [slots]
    for j in steps:
        answer = shift(message, "adapter", j)
        scaled_of.append(answer[:rows])
        numbers = answer[rows : rows + 2 * tag_rows].astype(jnp.int32)
        numbers = numbers[:tag_rows] * SPLIT + numbers[tag_rows:]
        slots_of.append(numbers.reshape(-1)[:rows])
    row_slots = jnp.stack(slots_of)
    slot_columns = row_slots.T

    def over_shares(matrix):
        columns = matrix.shape[1] // shares
        sent = [
            lax.dynamic_slice_in_dim(matrix, (share ^ k) * columns, columns, 1)
            for k in range(shares)
        ]
        return jnp.concatenate(
            [sent[0]] + [swap(sent[k], "tensor", k) for k in range(1, shares)]
        )

    own_ups = over_shares(adapter_up_weight.reshape(stored * rank, values))
    down_flat = after(adapter_down_weight.reshape(stored * rank, shares * width), own_ups)
    own_down = over_shares(down_flat)
    gated_ups = after(own_ups, own_down, *shared)

    pieces, position = [], 0
    for part in PIECES:
        piece_width = width // part
        others = tokens[:, position : position + piece_width]
        others = after(others, own_ups)
        pieces.append(
            (
                (position // piece_width, piece_width),
                [tokens] + [shift(others, "adapter", j) for j in steps],
            )
        )
        position += piece_width

    base_term = dot(tokens, frozen_value_weight, 1, 0).astype(jnp.bfloat16)

    column = jnp.arange(own * rank, dtype=jnp.int32)
    sent_slots = (side * shares + (share ^ (column // (stored * rank)))) * stored
    sent_slots += (column // rank) % stored
    sent_select = choose(column % rank, rank)
    part_local = (column % (own * piece)) // piece
    part_plane = column // (own * piece)
    part_plane = (part_plane % far) * near + part_plane // far
    part_ranks = part_plane * piece + column % piece
    part_slots = (side * own + part_local)[:, None]
    part_select = choose(part_ranks, rank).T

    back_part = fold_product(
        scaled_of,
        gated_ups,
        (0, value_width),
        sent_slots[None, :],
        slot_columns,
        rank,
        ADAPTER_SCALE,
        None,
        jnp.bfloat16,
    )
    back_part, base_term = lax.optimization_barrier((back_part, base_term))
    back_all = tensor_sum(back_part)
    back = back_all[:, :rank]
    for j in steps:
        back = back + shift(back_all[:, j * rank : (j + 1) * rank], "adapter", -j)


    base_share = scatter_columns(base_term)
    back_gate = back_all
    low_part = None
    parts_down = []
    for n, (block, lines) in enumerate(pieces):
        last = n == len(pieces) - 1

        def gradient():
            return weight_product(
                back_gate, row_slots, part_slots, part_select, lines, block, 1.0
            )

        if not last:
            parts_down.append(gradient())
            own_down = after(own_down, parts_down[-1])
        low_part = fold_product(
            lines,
            own_down,
            block,
            sent_slots[None, :],
            slot_columns,
            rank,
            1.0,
            low_part,
            jnp.bfloat16 if last else jnp.float32,
        )
        if last:
            low_part = tensor_sum(low_part, bits_below(shares)[:1])
        low_part, back_gate, base_share = lax.optimization_barrier(
            (low_part, back_gate, base_share)
        )
        if last:
            parts_down.append(gradient())
    bundle = rank // far
    by_rank = own_down.reshape(own, rank, width)
    rests = []
    for j in steps:
        for i in range(1, far):
            start = (plane // near + i) % far * bundle
            rest = lax.dynamic_slice_in_dim(by_rank, start, bundle, 1)
            rests.append(shift(rest.reshape(own * bundle, width), "adapter", j))

    def fold(part):
        half = part.shape[0] // near
        kept = lax.dynamic_slice_in_dim(part, close * half, half, 0)
        for j in range(1, near):
            away = lax.dynamic_slice_in_dim(part, ((close + j) % near) * half, half, 0)
            kept = add(kept, shift(away, "near", j))
        return kept

    def send(part):
        return exchange(part.reshape(far * shares, lot, part.shape[1]), ("far", "tensor"))

    parts_down = [fold(part) for part in parts_down]
    first = send(after(parts_down[0], *pieces[1][1][1:]))
    low_all = tensor_sum(low_part, bits_below(shares)[1:])
    up_part = weight_product(
        low_all, row_slots, part_slots, part_select, scaled_of, (0, value_width), ADAPTER_SCALE
    )
    last_width = parts_down[-1].shape[1]
    parts_down[-1] = jnp.concatenate([parts_down[-1], fold(up_part)], axis=1)
    parts_down[-1] = after(parts_down[-1], *rests)

    arrived = [first]
    for part in parts_down[1:]:
        arrived.append(send(after(part, arrived[-1])))
    grad_down, grad_up = total_product(arrived, far, shares, width, last_width, value_width)
    grad_down = grad_down.reshape(stored, piece, shares * width)
    grad_up = grad_up.reshape(stored, piece, values)

    addends = [base_share]
    for j in steps:
        theirs = output_product(
            [],
            low_all[:, j * rank : (j + 1) * rank],
            slots_of[j][:, None],
            sent_slots[None, :],
            sent_select,
            own_ups,
        )
        addends.append(shift(theirs, "adapter", -j))
    columns, selects, downs = [sent_slots[None, :]], [sent_select], [own_down]

    def block(weights, block_slots, block_ranks):
        columns.append(block_slots[None, :])
        selects.append(choose(block_ranks, rank))
        downs.append(weights)

    quarter_column = column[: own * piece]
    bundle_column = column[: own * bundle]
    for j in steps:
        away = (side - j) % sides
        for i, weights in enumerate(quarters[j - 1]):
            from_plane = plane - close + (close - i) % near
            block(
                weights,
                away * own + quarter_column // piece,
                from_plane * piece + quarter_column % piece,
            )
        for i in range(1, far):
            adapter = bundle_column // bundle
            block(
                rests[(j - 1) * (far - 1) + i - 1],
                (away * shares + (share ^ (adapter // stored))) * stored + adapter % stored,
                (plane // near + i) % far * bundle + bundle_column % bundle,
            )
    input_gradient = input_product(
        scaled,
        frozen_value_weight,
        back,
        slots[:, None],
        columns,
        selects,
        downs,
        max(LANES, 1024 // sides),
    )
    addends[0] = after(addends[0], input_gradient)
    mixed_out = output_product(
        addends, low_all[:, :rank], slots[:, None], sent_slots[None, :], sent_select, own_ups
    )
    return mixed_out, input_gradient, grad_down, grad_up


def solution(mesh):
    planes = mesh.shape["dp"]
    near = 2 if planes % 2 == 0 else 1
    split = Mesh(
        mesh.devices.reshape((planes // near, near) + mesh.devices.shape[1:]),
        ("far", "near") + tuple(mesh.axis_names[1:]),
    )
    dp = ("far", "near")
    lines = dp + ("adapter",)
    return jax.shard_map(
        shards,
        mesh=split,
        in_specs=(
            P(lines, "tensor"),
            P("tensor", None),
            P(("adapter", "tensor"), None, None),
            P(("adapter", "tensor"), None, None),
            P(lines, None),
            P(lines),
            P(lines, None),
            P(),
        ),
        out_specs=(
            P(lines, "tensor"),
            P(lines, "tensor"),
            P(("adapter", "tensor"), dp, None),
            P(("adapter", "tensor"), dp, None),
        ),
        check_vma=False,
    )
```

```python
import functools

import jax
import jax.numpy as jnp
from jax import lax
from jax.experimental import pallas as pl
from jax.experimental.pallas import tpu as pltpu
from jax.sharding import Mesh
from jax.sharding import PartitionSpec as P

ADAPTER_SCALE = 0.5
PIECES = (2, 4, 4)
SPLIT = 128
HINT = 1000
LANES = 128
VMEM = 56 * 1024 * 1024


def exchange(pieces, axes):
    return lax.all_to_all(pieces, axes, split_axis=0, concat_axis=0, tiled=True)


def shift(array, axis, step):
    size = lax.axis_size(axis)
    return lax.ppermute(array, axis, [(i, (i + step) % size) for i in range(size)])


def swap(array, axis, bit):
    return lax.ppermute(array, axis, [(i, i ^ bit) for i in range(lax.axis_size(axis))])


def after(value, *earlier):
    return lax.optimization_barrier((value,) + earlier)[0]


def add(a, b):
    return (a.astype(jnp.float32) + b.astype(jnp.float32)).astype(jnp.bfloat16)


def bits_below(size):
    return [1 << i for i in range(size.bit_length() - 1)]


def tensor_sum(total, bits=None):
    for bit in bits_below(lax.axis_size("tensor")) if bits is None else bits:
        total = add(total, swap(total, "tensor", bit))
    return total


def scatter_columns(term, gate=None):
    size = lax.axis_size("tensor")
    share = lax.axis_index("tensor")
    width = term.shape[1] // size
    blocks = [
        lax.dynamic_slice_in_dim(term, (share ^ i) * width, width, 1) for i in range(size)
    ]
    for bit in bits_below(size):
        kept = [i for i in range(size) if i % (2 * bit) == 0]
        if 2 * bit == size:
            blocks = after(blocks, gate)
        got = swap(jnp.concatenate([blocks[i ^ bit] for i in kept], axis=1), "tensor", bit)
        for n, i in enumerate(kept):
            blocks[i] = add(blocks[i], got[:, n * width : (n + 1) * width])
    return blocks[0]


def dot(a, b, ca, cb):
    return lax.dot_general(a, b, (((ca,), (cb,)), ((), ())), preferred_element_type=jnp.float32)


def call(body, grid, in_specs, out_spec, out_shape, operands, flops, scratch=()):
    moved = sum(x.size * x.dtype.itemsize for x in operands)
    return pl.pallas_call(
        body,
        grid=grid,
        in_specs=in_specs,
        out_specs=out_spec,
        out_shape=out_shape,
        scratch_shapes=list(scratch),
        compiler_params=pltpu.CompilerParams(vmem_limit_bytes=VMEM),
        cost_estimate=pl.CostEstimate(flops=flops // HINT, bytes_accessed=moved // HINT, transcendentals=0),
    )(*operands)


def whole(array):
    return pl.BlockSpec(array.shape, lambda i: (0,) * array.ndim)


def fold_body(count, rank, scale, *refs):
    lines, weight, column_slots, slots = refs[:count], refs[count], refs[count + 1], refs[count + 2]
    out = refs[-1]
    step = max(rank, LANES)
    results = []
    for n in range(count):
        full = dot(lines[n][...], weight[...], 1, 1)
        full = jnp.where(slots[:, n : n + 1] == column_slots[...], full, 0.0)
        total = full[:, :step]
        for i in range(step, full.shape[1], step):
            total += full[:, i : i + step]
        results.append(sum(total[:, i : i + rank] for i in range(0, step, rank)))
    result = scale * jnp.concatenate(results, axis=1)
    if len(refs) == count + 5:
        result += refs[count + 3][...]
    out[...] = result.astype(out.dtype)


def fold_product(lines, weight, block, column_slots, slots, rank, scale, before, dtype):
    count = len(lines)
    rows = slots.shape[0]
    tile = rows // 2
    offset, depth = block
    specs = [
        pl.BlockSpec((tile, depth), functools.partial(lambda o, i: (i, o), 0))
        if line.shape[1] == depth
        else pl.BlockSpec((tile, depth), lambda i: (i, offset))
        for line in lines
    ]
    specs.append(pl.BlockSpec((weight.shape[0], depth), lambda i: (0, offset)))
    specs.append(whole(column_slots))
    specs.append(pl.BlockSpec((tile, count), lambda i: (i, 0)))
    operands = list(lines) + [weight, column_slots, slots]
    out_spec = pl.BlockSpec((tile, count * rank), lambda i: (i, 0))
    if before is not None:
        specs.append(out_spec)
        operands.append(before)
    return call(
        functools.partial(fold_body, count, rank, scale),
        (2,),
        specs,
        out_spec,
        jax.ShapeDtypeStruct((rows, count * rank), dtype),
        operands,
        2 * count * rows * weight.shape[0] * depth,
    )


def weight_body(count, rank, scale, *refs):
    compact, row_slots, column_slots, select = refs[:4]
    lines, out, spread = refs[4 : 4 + count], refs[-2], refs[-1]

    @pl.when(pl.program_id(0) == 0)
    def _():
        for n in range(count):
            wide = dot(select[...], compact[:, n * rank : (n + 1) * rank], 1, 1)
            mine = column_slots[...] == row_slots[n : n + 1, :]
            spread[n] = jnp.where(mine, wide, 0.0).astype(jnp.bfloat16)

    total = dot(spread[0], lines[0][...], 1, 0)
    for n in range(1, count):
        total += dot(spread[n], lines[n][...], 1, 0)
    out[...] = (scale * total).astype(out.dtype)


def weight_product(compact, row_slots, column_slots, select, lines, block, scale):
    count = len(lines)
    rows = row_slots.shape[1]
    columns, rank = select.shape
    offset, width = block
    tile = min(width, 512)
    per = width // tile
    specs = [whole(x) for x in (compact, row_slots, column_slots, select)]
    for line in lines:
        skip = 0 if line.shape[1] == width else offset * per
        specs.append(pl.BlockSpec((rows, tile), functools.partial(lambda s, i: (0, s + i), skip)))
    return call(
        functools.partial(weight_body, count, rank, scale),
        (per,),
        specs,
        pl.BlockSpec((columns, tile), lambda i: (0, i)),
        jax.ShapeDtypeStruct((columns, width), jnp.bfloat16),
        [compact, row_slots, column_slots, select] + list(lines),
        2 * count * rows * columns * width,
        [pltpu.VMEM((count, columns, rows), jnp.bfloat16)],
    )


def piece_body(count, rank, has_before, *refs):
    compact, row_slots, part_slots, select, weight, column_slots, slots = refs[:7]
    lines = refs[7 : 7 + count]
    out_weight, out_low, spread, *fulls = refs[7 + count + has_before :]
    step = pl.program_id(0)

    @pl.when(step == 0)
    def _():
        for n in range(count):
            wide = dot(select[...], compact[:, n * rank : (n + 1) * rank], 1, 1)
            mine = part_slots[...] == row_slots[n : n + 1, :]
            spread[n] = jnp.where(mine, wide, 0.0).astype(jnp.bfloat16)
            if fulls:
                fulls[n][...] = dot(lines[n][...], weight[...], 1, 1)

    if fulls:

        @pl.when(step > 0)
        def _():
            for n in range(count):
                fulls[n][...] += dot(lines[n][...], weight[...], 1, 1)

    @pl.when(step == pl.num_programs(0) - 1)
    def _():
        block = max(rank, LANES)
        results = []
        for n in range(count):
            full = fulls[n][...] if fulls else dot(lines[n][...], weight[...], 1, 1)
            full = jnp.where(slots[:, n : n + 1] == column_slots[...], full, 0.0)
            total = full[:, :block]
            for i in range(block, full.shape[1], block):
                total += full[:, i : i + block]
            results.append(sum(total[:, i : i + rank] for i in range(0, block, rank)))
        result = jnp.concatenate(results, axis=1)
        if has_before:
            result += refs[7 + count][...]
        out_low[...] = result.astype(out_low.dtype)

    total = dot(spread[0], lines[0][...], 1, 0)
    for n in range(1, count):
        total += dot(spread[n], lines[n][...], 1, 0)
    out_weight[...] = total.astype(out_weight.dtype)


def piece_product(
    compact, row_slots, part_slots, select, weight, column_slots, slots, lines, block, before, dtype
):
    count = len(lines)
    rows = row_slots.shape[1]
    columns, rank = select.shape
    offset, width = block
    tile = min(width, 512)
    per = width // tile
    here = lambda i: (0, offset * per + i)
    small = [compact, row_slots, part_slots, select, column_slots, slots]
    specs = [whole(x) for x in small[:4]] + [pl.BlockSpec((columns, tile), here)]
    specs += [whole(x) for x in small[4:]]
    for line in lines:
        skip = 0 if line.shape[1] == width else offset * per
        specs.append(pl.BlockSpec((rows, tile), functools.partial(lambda s, i: (0, s + i), skip)))
    operands = small[:4] + [weight] + small[4:] + list(lines)
    if before is not None:
        specs.append(whole(before))
        operands.append(before)
    low = jax.ShapeDtypeStruct((rows, count * rank), dtype)
    return call(
        functools.partial(piece_body, count, rank, before is not None),
        (per,),
        specs,
        [pl.BlockSpec((columns, tile), lambda i: (0, i)), whole(low)],
        [jax.ShapeDtypeStruct((columns, width), jnp.bfloat16), low],
        operands,
        4 * count * rows * columns * width,
        [pltpu.VMEM((count, columns, rows), jnp.bfloat16)]
        + [pltpu.VMEM((rows, columns), jnp.float32)] * (count if per > 1 else 0),
    )


def input_body(count, *refs):
    scaled, frozen, compact, slots = refs[:4]
    columns, selects, downs = (refs[4 + i * count : 4 + (i + 1) * count] for i in range(3))
    out, spreads = refs[-1 - count], refs[-count:]

    @pl.when(pl.program_id(0) == 0)
    def _():
        for n in range(count):
            wide = dot(compact[...], selects[n][...], 1, 0)
            mine = slots[:, :1] == columns[n][...]
            spreads[n][...] = jnp.where(mine, wide, 0.0).astype(jnp.bfloat16)

    total = dot(scaled[...], frozen[...], 1, 1)
    for n in range(count):
        total += dot(spreads[n][...], downs[n][...], 1, 0)
    out[...] = total.astype(out.dtype)


def input_product(scaled, frozen, compact, slots, columns, selects, downs, tile):
    count = len(downs)
    rows, values = scaled.shape
    width = downs[0].shape[1]
    specs = [whole(scaled), pl.BlockSpec((tile, values), lambda i: (i, 0))]
    specs += [whole(x) for x in [compact, slots] + columns + selects]
    specs += [pl.BlockSpec((x.shape[0], tile), lambda i: (0, i)) for x in downs]
    return call(
        functools.partial(input_body, count),
        (width // tile,),
        specs,
        pl.BlockSpec((rows, tile), lambda i: (0, i)),
        jax.ShapeDtypeStruct((rows, width), jnp.bfloat16),
        [scaled, frozen, compact, slots] + columns + selects + list(downs),
        2 * rows * width * (values + sum(x.shape[0] for x in downs)),
        [pltpu.VMEM((rows, x.shape[0]), jnp.bfloat16) for x in downs],
    )


def output_body(count, which, rank, *refs):
    compact, slots, column_slots, select, ups = refs[count : count + 5]
    out = refs[-1]
    wide = dot(compact[:, which * rank : (which + 1) * rank], select[...], 1, 0)
    mine = slots[:, which : which + 1] == column_slots[...]
    spread = jnp.where(mine, wide, 0.0).astype(jnp.bfloat16)
    result = ADAPTER_SCALE * dot(spread, ups[...], 1, 0)
    for addend in refs[:count]:
        result += addend[...].astype(jnp.float32)
    out[...] = result.astype(out.dtype)


def output_product(addends, which, compact, slots, column_slots, select, ups):
    rows, width = compact.shape[0], ups.shape[1]
    tile = rows // 2
    line = lambda i: (i, 0)
    operands = list(addends) + [compact, slots]
    specs = [pl.BlockSpec((tile, x.shape[1]), line) for x in operands]
    operands += [column_slots, select, ups]
    specs += [whole(x) for x in operands[-3:]]
    return call(
        functools.partial(output_body, len(addends), which, select.shape[0]),
        (rows // tile,),
        specs,
        pl.BlockSpec((tile, width), line),
        jax.ShapeDtypeStruct((rows, width), jnp.bfloat16),
        operands,
        2 * rows * width * ups.shape[0],
    )


def total_body(shares, width, last_width, value_width, *refs):
    out_down, out_up = refs[-2:]
    position = 0
    for ref in refs[:-2]:
        last = ref is refs[-3]
        columns = last_width if last else ref.shape[2]
        for share in range(shares):
            total = sum(
                ref[source].astype(jnp.float32) for source in range(share, ref.shape[0], shares)
            )
            start = share * width + position
            out_down[:, start : start + columns] = total[:, :columns].astype(jnp.bfloat16)
            if last:
                start = share * value_width
                out_up[:, start : start + value_width] = total[:, columns:].astype(jnp.bfloat16)
        position += columns


def total_product(arrived, shares, width, last_width, value_width):
    lot = arrived[0].shape[1]
    shapes = [
        jax.ShapeDtypeStruct((lot, shares * columns), jnp.bfloat16)
        for columns in (width, value_width)
    ]
    return call(
        functools.partial(total_body, shares, width, last_width, value_width),
        (1,),
        [whole(x) for x in arrived],
        [whole(x) for x in shapes],
        shapes,
        arrived,
        1000,
    )


def choose(ranks, rank):
    return (jnp.arange(rank, dtype=jnp.int32)[:, None] == ranks[None, :]).astype(jnp.bfloat16)


def shards(
    tokens,
    frozen_value_weight,
    adapter_down_weight,
    adapter_up_weight,
    cotangent,
    language_pair_index,
    language_pair_counts,
    adapter_owner_table,
):
    sides = lax.axis_size("adapter")
    shares = lax.axis_size("tensor")
    far, near = lax.axis_size("far"), lax.axis_size("near")
    planes = far * near
    side = lax.axis_index("adapter")
    share = lax.axis_index("tensor")
    plane = lax.axis_index(("far", "near"))
    close = lax.axis_index("near")
    rows, width = tokens.shape
    stored, rank, _ = adapter_down_weight.shape
    values = cotangent.shape[1]
    value_width = values // shares
    own = shares * stored
    piece = rank // planes
    lot = stored * piece
    steps = range(1, sides)

    quarter = lax.dynamic_slice_in_dim(adapter_down_weight, plane * piece, piece, 1)
    quarter = quarter.reshape(lot, shares * width)
    parcel = jnp.stack([quarter[:, s * width : (s + 1) * width] for s in range(shares)])
    parcel = jnp.broadcast_to(parcel[None], (sides,) + parcel.shape)
    parcel = parcel.reshape(sides * shares, lot, width)
    got = exchange(parcel, ("adapter", "tensor"))

    quarters = []
    for j in steps:
        block = lax.dynamic_slice(
            got, (((side - j) % sides) * shares, 0, 0), (shares, lot, width)
        ).reshape(own * piece, width)
        quarters.append([block] + [shift(block, "near", i) for i in range(1, near)])
    shared = [block for blocks in quarters for block in blocks]
    spread_far = [[shift(q[0], "far", i) for i in range(1, far)] for q in quarters]

    pairs = jnp.arange(adapter_owner_table.shape[0], dtype=jnp.int32)
    matches = language_pair_index[:, None] == pairs[None, :]
    slots = jnp.sum(jnp.where(matches, adapter_owner_table[None, :], 0), axis=1)
    row_counts = jnp.sum(jnp.where(matches, language_pair_counts[0][None, :], 0), axis=1)
    row_weight = 1.0 / row_counts.astype(jnp.float32)
    scaled = (cotangent.astype(jnp.float32) * row_weight[:, None]).astype(jnp.bfloat16)
    scaled_part = lax.dynamic_slice_in_dim(scaled, share * value_width, value_width, 1)

    tag_rows = -(-rows // value_width)
    tags = jnp.pad(slots, (0, tag_rows * value_width - rows)).reshape(tag_rows, value_width)
    tags = jnp.concatenate([tags // SPLIT, tags % SPLIT]).astype(jnp.bfloat16)
    tags = jnp.pad(tags, ((0, -2 * tag_rows % 16), (0, 0)))
    message = after(jnp.concatenate([scaled_part, tags]), parcel)
    scaled_of, slots_of = [scaled_part], [slots]
    for j in steps:
        answer = shift(message, "adapter", j)
        scaled_of.append(answer[:rows])
        numbers = answer[rows : rows + 2 * tag_rows].astype(jnp.int32)
        numbers = numbers[:tag_rows] * SPLIT + numbers[tag_rows:]
        slots_of.append(numbers.reshape(-1)[:rows])
    row_slots = jnp.stack(slots_of)
    slot_columns = row_slots.T

    def over_shares(matrix):
        columns = matrix.shape[1] // shares
        sent = [
            lax.dynamic_slice_in_dim(matrix, (share ^ k) * columns, columns, 1)
            for k in range(shares)
        ]
        return jnp.concatenate(
            [sent[0]] + [swap(sent[k], "tensor", k) for k in range(1, shares)]
        )

    own_ups = over_shares(adapter_up_weight.reshape(stored * rank, values))
    down_flat = after(adapter_down_weight.reshape(stored * rank, shares * width), own_ups)
    own_down = over_shares(down_flat)
    gated_ups = after(own_ups, own_down, *shared, *[b for blocks in spread_far for b in blocks])

    pieces, position = [], 0
    for part in PIECES:
        piece_width = width // part
        others = tokens[:, position : position + piece_width]
        others = after(others, own_ups)
        pieces.append(
            (
                (position // piece_width, piece_width),
                [tokens] + [shift(others, "adapter", j) for j in steps],
            )
        )
        position += piece_width

    base_term = dot(tokens, frozen_value_weight, 1, 0).astype(jnp.bfloat16)

    column = jnp.arange(own * rank, dtype=jnp.int32)
    sent_slots = (side * shares + (share ^ (column // (stored * rank)))) * stored
    sent_slots += (column // rank) % stored
    sent_select = choose(column % rank, rank)
    part_local = (column % (own * piece)) // piece
    part_plane = column // (own * piece)
    part_plane = (part_plane % far) * near + part_plane // far
    part_ranks = part_plane * piece + column % piece
    part_slots = (side * own + part_local)[:, None]
    part_select = choose(part_ranks, rank).T

    columns, selects = [sent_slots[None, :]], [sent_select]
    quarter_column = column[: own * piece]
    adapter = quarter_column // piece
    per = (far - 1) * (near - 1)
    for j in steps:
        away = (side - j) % sides
        mine = plane // near
        stored_order = away * own + adapter
        sent_order = (away * shares + (share ^ (adapter // stored))) * stored + adapter % stored
        blocks = [(stored_order, mine * near + (close - i) % near) for i in range(near)]
        blocks += [(stored_order, (mine - i) % far * near + close) for i in range(1, far)]
        blocks += [
            (sent_order, (mine + i) % far * near + (close + k) % near)
            for i in range(1, far)
            for k in range(1, near)
        ]
        for block_slots, from_plane in blocks:
            columns.append(block_slots[None, :])
            selects.append(choose(from_plane * piece + quarter_column % piece, rank))
    tables = (part_slots, part_select, sent_slots, sent_select, columns, selects, slot_columns)
    gated_ups, tables = lax.optimization_barrier((gated_ups, tables))
    part_slots, part_select, sent_slots, sent_select, columns, selects, slot_columns = tables

    back_part = fold_product(
        scaled_of,
        gated_ups,
        (0, value_width),
        sent_slots[None, :],
        slot_columns,
        rank,
        ADAPTER_SCALE,
        None,
        jnp.bfloat16,
    )
    back_part, base_term = lax.optimization_barrier((back_part, base_term))
    back_all = tensor_sum(back_part)
    replies = [shift(back_all[:, j * rank : (j + 1) * rank], "adapter", -j) for j in steps]


    back_gate = back_all
    groups = [slice(g, min(g + 2, sides)) for g in range(0, sides, 2)]
    lows = [None] * len(groups)
    parts_down = []
    for n, (block, lines) in enumerate(pieces):
        last = n == len(pieces) - 1
        parts = []
        for g, group in enumerate(groups):
            part, lows[g] = piece_product(
                back_gate[:, group.start * rank : group.stop * rank],
                row_slots[group],
                part_slots,
                part_select,
                own_down,
                sent_slots[None, :],
                slot_columns[:, group],
                lines[group],
                block,
                lows[g],
                jnp.bfloat16 if last else jnp.float32,
            )
            parts.append(part)
        parts_down.append(functools.reduce(add, parts))
        if last:
            low_part = tensor_sum(jnp.concatenate(lows, axis=1), bits_below(shares)[:1])
        lows, back_gate = lax.optimization_barrier((lows, back_gate))
    by_rank = own_down.reshape(own, rank, width)
    rests = []
    for j in steps:
        for i in range(1, far):
            for k in range(1, near):
                start = ((plane // near + i) % far * near + (close + k) % near) * piece
                rest = lax.dynamic_slice_in_dim(by_rank, start, piece, 1)
                rests.append(shift(rest.reshape(own * piece, width), "adapter", j))

    def fold_start(part):
        half = part.shape[0] // near
        pieces_of = [
            lax.dynamic_slice_in_dim(part, ((close + j) % near) * half, half, 0)
            for j in range(near)
        ]
        return [pieces_of[0]] + [shift(pieces_of[j], "near", j) for j in range(1, near)]

    def fold_end(parts):
        return functools.reduce(add, parts)

    def send(part, axes):
        size = lax.axis_size(axes)
        return exchange(part.reshape(size, lot, part.shape[1]), axes)

    first = send(parts_down[0], ("near", "far", "tensor"))
    started = [fold_start(part) for part in parts_down[1:]]
    low_all = tensor_sum(low_part, bits_below(shares)[1:])
    base_share = scatter_columns(base_term, low_all)
    up_part = weight_product(
        low_all, row_slots, part_slots, part_select, scaled_of, (0, value_width), ADAPTER_SCALE
    )
    last_width = sum(part.shape[1] for part in parts_down[1:])
    up_start = fold_start(up_part)
    up_start, started, replies = lax.optimization_barrier((up_start, started, replies))
    back = sum(replies, back_all[:, :rank])
    folded = jnp.concatenate([fold_end(parts) for parts in started + [up_start]], axis=1)
    second = send(after(folded, first, base_share, *rests), ("far", "tensor"))
    arrived = [first, second]
    grad_down, grad_up = total_product(arrived, shares, width, last_width, value_width)
    grad_down = grad_down.reshape(stored, piece, shares * width)
    grad_up = grad_up.reshape(stored, piece, values)

    addends = [base_share]
    for j in steps:
        theirs = output_product(
            [],
            j,
            low_all,
            slot_columns,
            sent_slots[None, :],
            sent_select,
            own_ups,
        )
        addends.append(shift(theirs, "adapter", -j))
    downs = [own_down] + [block for n in range(len(steps)) for block in (
        quarters[n] + spread_far[n] + rests[n * per : (n + 1) * per]
    )]
    input_gradient = input_product(
        scaled,
        frozen_value_weight,
        back,
        slot_columns,
        columns,
        selects,
        downs,
        max(LANES, 1024 // sides),
    )
    addends[0] = after(addends[0], input_gradient)
    mixed_out = output_product(
        addends, 0, low_all, slot_columns, sent_slots[None, :], sent_select, own_ups
    )
    return mixed_out, input_gradient, grad_down, grad_up


def solution(mesh):
    planes = mesh.shape["dp"]
    near = 2 if planes % 2 == 0 else 1
    split = Mesh(
        mesh.devices.reshape((planes // near, near) + mesh.devices.shape[1:]),
        ("far", "near") + tuple(mesh.axis_names[1:]),
    )
    dp = ("far", "near")
    lines = dp + ("adapter",)
    return jax.shard_map(
        shards,
        mesh=split,
        in_specs=(
            P(lines, "tensor"),
            P("tensor", None),
            P(("adapter", "tensor"), None, None),
            P(("adapter", "tensor"), None, None),
            P(lines, None),
            P(lines),
            P(lines, None),
            P(),
        ),
        out_specs=(
            P(lines, "tensor"),
            P(lines, "tensor"),
            P(("adapter", "tensor"), dp, None),
            P(("adapter", "tensor"), dp, None),
        ),
        check_vma=False,
    )
```

```python
import functools

import jax
import jax.numpy as jnp
from jax import lax
from jax.experimental import pallas as pl
from jax.experimental.pallas import tpu as pltpu
from jax.sharding import Mesh
from jax.sharding import PartitionSpec as P

ADAPTER_SCALE = 0.5
PIECES = (2, 4, 4)
SPLIT = 128
HINT = 1000
LANES = 128
VMEM = 56 * 1024 * 1024


def exchange(pieces, axes):
    return lax.all_to_all(pieces, axes, split_axis=0, concat_axis=0, tiled=True)


def shift(array, axis, step):
    size = lax.axis_size(axis)
    return lax.ppermute(array, axis, [(i, (i + step) % size) for i in range(size)])


def swap(array, axis, bit):
    return lax.ppermute(array, axis, [(i, i ^ bit) for i in range(lax.axis_size(axis))])


def after(value, *earlier):
    return lax.optimization_barrier((value,) + earlier)[0]


def add(a, b):
    return (a.astype(jnp.float32) + b.astype(jnp.float32)).astype(jnp.bfloat16)


def bits_below(size):
    return [1 << i for i in range(size.bit_length() - 1)]


def tensor_sum(total, bits=None):
    for bit in bits_below(lax.axis_size("tensor")) if bits is None else bits:
        total = add(total, swap(total, "tensor", bit))
    return total


def scatter_columns(term, gate=None):
    size = lax.axis_size("tensor")
    share = lax.axis_index("tensor")
    width = term.shape[1] // size
    blocks = [
        lax.dynamic_slice_in_dim(term, (share ^ i) * width, width, 1) for i in range(size)
    ]
    for bit in bits_below(size):
        kept = [i for i in range(size) if i % (2 * bit) == 0]
        if 2 * bit == size:
            blocks = after(blocks, gate)
        got = swap(jnp.concatenate([blocks[i ^ bit] for i in kept], axis=1), "tensor", bit)
        for n, i in enumerate(kept):
            blocks[i] = add(blocks[i], got[:, n * width : (n + 1) * width])
    return blocks[0]


def dot(a, b, ca, cb):
    return lax.dot_general(a, b, (((ca,), (cb,)), ((), ())), preferred_element_type=jnp.float32)


def call(body, grid, in_specs, out_spec, out_shape, operands, flops, scratch=()):
    moved = sum(x.size * x.dtype.itemsize for x in operands)
    return pl.pallas_call(
        body,
        grid=grid,
        in_specs=in_specs,
        out_specs=out_spec,
        out_shape=out_shape,
        scratch_shapes=list(scratch),
        compiler_params=pltpu.CompilerParams(vmem_limit_bytes=VMEM),
        cost_estimate=pl.CostEstimate(flops=flops // HINT, bytes_accessed=moved // HINT, transcendentals=0),
    )(*operands)


def whole(array):
    return pl.BlockSpec(array.shape, lambda i: (0,) * array.ndim)


def fold_body(count, rank, scale, *refs):
    lines, weight, column_slots, slots = refs[:count], refs[count], refs[count + 1], refs[count + 2]
    out = refs[-1]
    step = max(rank, LANES)
    results = []
    for n in range(count):
        full = dot(lines[n][...], weight[...], 1, 1)
        full = jnp.where(slots[:, n : n + 1] == column_slots[...], full, 0.0)
        total = full[:, :step]
        for i in range(step, full.shape[1], step):
            total += full[:, i : i + step]
        results.append(sum(total[:, i : i + rank] for i in range(0, step, rank)))
    result = scale * jnp.concatenate(results, axis=1)
    if len(refs) == count + 5:
        result += refs[count + 3][...]
    out[...] = result.astype(out.dtype)


def fold_product(lines, weight, block, column_slots, slots, rank, scale, before, dtype):
    count = len(lines)
    rows = slots.shape[0]
    tile = rows // 2
    offset, depth = block
    specs = [
        pl.BlockSpec((tile, depth), functools.partial(lambda o, i: (i, o), 0))
        if line.shape[1] == depth
        else pl.BlockSpec((tile, depth), lambda i: (i, offset))
        for line in lines
    ]
    specs.append(pl.BlockSpec((weight.shape[0], depth), lambda i: (0, offset)))
    specs.append(whole(column_slots))
    specs.append(pl.BlockSpec((tile, count), lambda i: (i, 0)))
    operands = list(lines) + [weight, column_slots, slots]
    out_spec = pl.BlockSpec((tile, count * rank), lambda i: (i, 0))
    if before is not None:
        specs.append(out_spec)
        operands.append(before)
    return call(
        functools.partial(fold_body, count, rank, scale),
        (2,),
        specs,
        out_spec,
        jax.ShapeDtypeStruct((rows, count * rank), dtype),
        operands,
        2 * count * rows * weight.shape[0] * depth,
    )


def weight_body(count, rank, scale, *refs):
    compact, row_slots, column_slots, select = refs[:4]
    lines, out, spread = refs[4 : 4 + count], refs[-2], refs[-1]

    @pl.when(pl.program_id(0) == 0)
    def _():
        for n in range(count):
            wide = dot(select[...], compact[:, n * rank : (n + 1) * rank], 1, 1)
            mine = column_slots[...] == row_slots[n : n + 1, :]
            spread[n] = jnp.where(mine, wide, 0.0).astype(jnp.bfloat16)

    total = dot(spread[0], lines[0][...], 1, 0)
    for n in range(1, count):
        total += dot(spread[n], lines[n][...], 1, 0)
    out[...] = (scale * total).astype(out.dtype)


def weight_product(compact, row_slots, column_slots, select, lines, block, scale):
    count = len(lines)
    rows = row_slots.shape[1]
    columns, rank = select.shape
    offset, width = block
    tile = min(width, 512)
    per = width // tile
    specs = [whole(x) for x in (compact, row_slots, column_slots, select)]
    for line in lines:
        skip = 0 if line.shape[1] == width else offset * per
        specs.append(pl.BlockSpec((rows, tile), functools.partial(lambda s, i: (0, s + i), skip)))
    return call(
        functools.partial(weight_body, count, rank, scale),
        (per,),
        specs,
        pl.BlockSpec((columns, tile), lambda i: (0, i)),
        jax.ShapeDtypeStruct((columns, width), jnp.bfloat16),
        [compact, row_slots, column_slots, select] + list(lines),
        2 * count * rows * columns * width,
        [pltpu.VMEM((count, columns, rows), jnp.bfloat16)],
    )


def piece_body(count, rank, has_before, *refs):
    compact, row_slots, part_slots, select, weight, column_slots, slots = refs[:7]
    lines = refs[7 : 7 + count]
    out_weight, out_low, spread, *fulls = refs[7 + count + has_before :]
    step = pl.program_id(0)

    @pl.when(step == 0)
    def _():
        for n in range(count):
            wide = dot(select[...], compact[:, n * rank : (n + 1) * rank], 1, 1)
            mine = part_slots[...] == row_slots[n : n + 1, :]
            spread[n] = jnp.where(mine, wide, 0.0).astype(jnp.bfloat16)
            if fulls:
                fulls[n][...] = dot(lines[n][...], weight[...], 1, 1)

    if fulls:

        @pl.when(step > 0)
        def _():
            for n in range(count):
                fulls[n][...] += dot(lines[n][...], weight[...], 1, 1)

    @pl.when(step == pl.num_programs(0) - 1)
    def _():
        block = max(rank, LANES)
        results = []
        for n in range(count):
            full = fulls[n][...] if fulls else dot(lines[n][...], weight[...], 1, 1)
            full = jnp.where(slots[:, n : n + 1] == column_slots[...], full, 0.0)
            total = full[:, :block]
            for i in range(block, full.shape[1], block):
                total += full[:, i : i + block]
            results.append(sum(total[:, i : i + rank] for i in range(0, block, rank)))
        result = jnp.concatenate(results, axis=1)
        if has_before:
            result += refs[7 + count][...]
        out_low[...] = result.astype(out_low.dtype)

    total = dot(spread[0], lines[0][...], 1, 0)
    for n in range(1, count):
        total += dot(spread[n], lines[n][...], 1, 0)
    out_weight[...] = total.astype(out_weight.dtype)


def piece_product(
    compact, row_slots, part_slots, select, weight, column_slots, slots, lines, block, before, dtype
):
    count = len(lines)
    rows = row_slots.shape[1]
    columns, rank = select.shape
    offset, width = block
    tile = min(width, 512)
    per = width // tile
    here = lambda i: (0, offset * per + i)
    small = [compact, row_slots, part_slots, select, column_slots, slots]
    specs = [whole(x) for x in small[:4]] + [pl.BlockSpec((columns, tile), here)]
    specs += [whole(x) for x in small[4:]]
    for line in lines:
        skip = 0 if line.shape[1] == width else offset * per
        specs.append(pl.BlockSpec((rows, tile), functools.partial(lambda s, i: (0, s + i), skip)))
    operands = small[:4] + [weight] + small[4:] + list(lines)
    if before is not None:
        specs.append(whole(before))
        operands.append(before)
    low = jax.ShapeDtypeStruct((rows, count * rank), dtype)
    return call(
        functools.partial(piece_body, count, rank, before is not None),
        (per,),
        specs,
        [pl.BlockSpec((columns, tile), lambda i: (0, i)), whole(low)],
        [jax.ShapeDtypeStruct((columns, width), jnp.bfloat16), low],
        operands,
        4 * count * rows * columns * width,
        [pltpu.VMEM((count, columns, rows), jnp.bfloat16)]
        + [pltpu.VMEM((rows, columns), jnp.float32)] * (count if per > 1 else 0),
    )


def input_body(count, *refs):
    scaled, frozen, compact, slots = refs[:4]
    columns, selects, downs = (refs[4 + i * count : 4 + (i + 1) * count] for i in range(3))
    out, spreads = refs[-1 - count], refs[-count:]

    @pl.when(pl.program_id(0) == 0)
    def _():
        for n in range(count):
            wide = dot(compact[...], selects[n][...], 1, 0)
            mine = slots[:, :1] == columns[n][...]
            spreads[n][...] = jnp.where(mine, wide, 0.0).astype(jnp.bfloat16)

    total = dot(scaled[...], frozen[...], 1, 1)
    for n in range(count):
        total += dot(spreads[n][...], downs[n][...], 1, 0)
    out[...] = total.astype(out.dtype)


def input_product(scaled, frozen, compact, slots, columns, selects, downs, tile):
    count = len(downs)
    rows, values = scaled.shape
    width = downs[0].shape[1]
    specs = [whole(scaled), pl.BlockSpec((tile, values), lambda i: (i, 0))]
    specs += [whole(x) for x in [compact, slots] + columns + selects]
    specs += [pl.BlockSpec((x.shape[0], tile), lambda i: (0, i)) for x in downs]
    return call(
        functools.partial(input_body, count),
        (width // tile,),
        specs,
        pl.BlockSpec((rows, tile), lambda i: (0, i)),
        jax.ShapeDtypeStruct((rows, width), jnp.bfloat16),
        [scaled, frozen, compact, slots] + columns + selects + list(downs),
        2 * rows * width * (values + sum(x.shape[0] for x in downs)),
        [pltpu.VMEM((rows, x.shape[0]), jnp.bfloat16) for x in downs],
    )


def output_body(count, which, rank, *refs):
    compact, slots, column_slots, select, ups = refs[count : count + 5]
    out = refs[-1]
    wide = dot(compact[:, which * rank : (which + 1) * rank], select[...], 1, 0)
    mine = slots[:, which : which + 1] == column_slots[...]
    spread = jnp.where(mine, wide, 0.0).astype(jnp.bfloat16)
    result = ADAPTER_SCALE * dot(spread, ups[...], 1, 0)
    for addend in refs[:count]:
        result += addend[...].astype(jnp.float32)
    out[...] = result.astype(out.dtype)


def output_product(addends, which, compact, slots, column_slots, select, ups):
    rows, width = compact.shape[0], ups.shape[1]
    tile = rows // 2
    line = lambda i: (i, 0)
    operands = list(addends) + [compact, slots]
    specs = [pl.BlockSpec((tile, x.shape[1]), line) for x in operands]
    operands += [column_slots, select, ups]
    specs += [whole(x) for x in operands[-3:]]
    return call(
        functools.partial(output_body, len(addends), which, select.shape[0]),
        (rows // tile,),
        specs,
        pl.BlockSpec((tile, width), line),
        jax.ShapeDtypeStruct((rows, width), jnp.bfloat16),
        operands,
        2 * rows * width * ups.shape[0],
    )


def total_body(shares, width, last_width, value_width, *refs):
    out_down, out_up = refs[-2:]
    position = 0
    for ref in refs[:-2]:
        last = ref is refs[-3]
        columns = last_width if last else ref.shape[2]
        for share in range(shares):
            total = sum(
                ref[source].astype(jnp.float32) for source in range(share, ref.shape[0], shares)
            )
            start = share * width + position
            out_down[:, start : start + columns] = total[:, :columns].astype(jnp.bfloat16)
            if last:
                start = share * value_width
                out_up[:, start : start + value_width] = total[:, columns:].astype(jnp.bfloat16)
        position += columns


def total_product(arrived, shares, width, last_width, value_width):
    lot = arrived[0].shape[1]
    shapes = [
        jax.ShapeDtypeStruct((lot, shares * columns), jnp.bfloat16)
        for columns in (width, value_width)
    ]
    return call(
        functools.partial(total_body, shares, width, last_width, value_width),
        (1,),
        [whole(x) for x in arrived],
        [whole(x) for x in shapes],
        shapes,
        arrived,
        1000,
    )


def choose(ranks, rank):
    return (jnp.arange(rank, dtype=jnp.int32)[:, None] == ranks[None, :]).astype(jnp.bfloat16)


def shards(
    tokens,
    frozen_value_weight,
    adapter_down_weight,
    adapter_up_weight,
    cotangent,
    language_pair_index,
    language_pair_counts,
    adapter_owner_table,
):
    sides = lax.axis_size("adapter")
    shares = lax.axis_size("tensor")
    far, near = lax.axis_size("far"), lax.axis_size("near")
    planes = far * near
    side = lax.axis_index("adapter")
    share = lax.axis_index("tensor")
    plane = lax.axis_index(("far", "near"))
    close = lax.axis_index("near")
    rows, width = tokens.shape
    stored, rank, _ = adapter_down_weight.shape
    values = cotangent.shape[1]
    value_width = values // shares
    own = shares * stored
    piece = rank // planes
    lot = stored * piece
    steps = range(1, sides)

    quarter = lax.dynamic_slice_in_dim(adapter_down_weight, plane * piece, piece, 1)
    quarter = quarter.reshape(lot, shares * width)
    parcel = jnp.stack([quarter[:, s * width : (s + 1) * width] for s in range(shares)])
    parcel = jnp.broadcast_to(parcel[None], (sides,) + parcel.shape)
    parcel = parcel.reshape(sides * shares, lot, width)
    got = exchange(parcel, ("adapter", "tensor"))

    quarters = []
    for j in steps:
        block = lax.dynamic_slice(
            got, (((side - j) % sides) * shares, 0, 0), (shares, lot, width)
        ).reshape(own * piece, width)
        quarters.append([block] + [shift(block, "near", i) for i in range(1, near)])
    shared = [block for blocks in quarters for block in blocks]
    spread_far = [[shift(q[0], "far", i) for i in range(1, far)] for q in quarters]

    pairs = jnp.arange(adapter_owner_table.shape[0], dtype=jnp.int32)
    matches = language_pair_index[:, None] == pairs[None, :]
    slots = jnp.sum(jnp.where(matches, adapter_owner_table[None, :], 0), axis=1)
    row_counts = jnp.sum(jnp.where(matches, language_pair_counts[0][None, :], 0), axis=1)
    row_weight = 1.0 / row_counts.astype(jnp.float32)
    scaled = (cotangent.astype(jnp.float32) * row_weight[:, None]).astype(jnp.bfloat16)
    scaled_part = lax.dynamic_slice_in_dim(scaled, share * value_width, value_width, 1)

    tag_rows = -(-rows // value_width)
    tags = jnp.pad(slots, (0, tag_rows * value_width - rows)).reshape(tag_rows, value_width)
    tags = jnp.concatenate([tags // SPLIT, tags % SPLIT]).astype(jnp.bfloat16)
    tags = jnp.pad(tags, ((0, -2 * tag_rows % 16), (0, 0)))
    message = after(jnp.concatenate([scaled_part, tags]), parcel)
    scaled_of, slots_of = [scaled_part], [slots]
    for j in steps:
        answer = shift(message, "adapter", j)
        scaled_of.append(answer[:rows])
        numbers = answer[rows : rows + 2 * tag_rows].astype(jnp.int32)
        numbers = numbers[:tag_rows] * SPLIT + numbers[tag_rows:]
        slots_of.append(numbers.reshape(-1)[:rows])
    row_slots = jnp.stack(slots_of)
    slot_columns = row_slots.T

    def over_shares(matrix):
        columns = matrix.shape[1] // shares
        sent = [
            lax.dynamic_slice_in_dim(matrix, (share ^ k) * columns, columns, 1)
            for k in range(shares)
        ]
        return jnp.concatenate(
            [sent[0]] + [swap(sent[k], "tensor", k) for k in range(1, shares)]
        )

    own_ups = over_shares(adapter_up_weight.reshape(stored * rank, values))
    down_flat = after(adapter_down_weight.reshape(stored * rank, shares * width), own_ups)
    own_down = over_shares(down_flat)
    gated_ups = after(own_ups, got)

    pieces, position = [], 0
    for part in PIECES:
        piece_width = width // part
        others = tokens[:, position : position + piece_width]
        others = after(others, own_ups)
        pieces.append(
            (
                (position // piece_width, piece_width),
                [tokens] + [shift(others, "adapter", j) for j in steps],
            )
        )
        position += piece_width

    base_term = dot(tokens, frozen_value_weight, 1, 0).astype(jnp.bfloat16)

    column = jnp.arange(own * rank, dtype=jnp.int32)
    sent_slots = (side * shares + (share ^ (column // (stored * rank)))) * stored
    sent_slots += (column // rank) % stored
    sent_select = choose(column % rank, rank)
    part_local = (column % (own * piece)) // piece
    part_plane = column // (own * piece)
    part_plane = (part_plane % far) * near + part_plane // far
    part_ranks = part_plane * piece + column % piece
    part_slots = (side * own + part_local)[:, None]
    part_select = choose(part_ranks, rank).T

    columns, selects = [sent_slots[None, :]], [sent_select]
    quarter_column = column[: own * piece]
    adapter = quarter_column // piece
    per = (far - 1) * (near - 1)
    for j in steps:
        away = (side - j) % sides
        mine = plane // near
        stored_order = away * own + adapter
        sent_order = (away * shares + (share ^ (adapter // stored))) * stored + adapter % stored
        blocks = [(stored_order, mine * near + (close - i) % near) for i in range(near)]
        blocks += [(stored_order, (mine - i) % far * near + close) for i in range(1, far)]
        blocks += [
            (sent_order, (mine + i) % far * near + (close + k) % near)
            for i in range(1, far)
            for k in range(1, near)
        ]
        for block_slots, from_plane in blocks:
            columns.append(block_slots[None, :])
            selects.append(choose(from_plane * piece + quarter_column % piece, rank))
    tables = (part_slots, part_select, sent_slots, sent_select, columns, selects, slot_columns)
    gated_ups, tables = lax.optimization_barrier((gated_ups, tables))
    part_slots, part_select, sent_slots, sent_select, columns, selects, slot_columns = tables

    back_part = fold_product(
        scaled_of,
        gated_ups,
        (0, value_width),
        sent_slots[None, :],
        slot_columns,
        rank,
        ADAPTER_SCALE,
        None,
        jnp.bfloat16,
    )
    back_part, base_term = lax.optimization_barrier((back_part, base_term))
    far_blocks = [block for blocks in spread_far for block in blocks]
    back_part = after(back_part, own_down, *shared, *far_blocks, *pieces[0][1][1:])
    back_all = tensor_sum(back_part)
    replies = [shift(back_all[:, j * rank : (j + 1) * rank], "adapter", -j) for j in steps]


    back_gate = back_all
    groups = [slice(g, min(g + 2, sides)) for g in range(0, sides, 2)]
    lows = [None] * len(groups)
    parts_down = []
    for n, (block, lines) in enumerate(pieces):
        last = n == len(pieces) - 1
        parts = []
        for g, group in enumerate(groups):
            part, lows[g] = piece_product(
                back_gate[:, group.start * rank : group.stop * rank],
                row_slots[group],
                part_slots,
                part_select,
                own_down,
                sent_slots[None, :],
                slot_columns[:, group],
                lines[group],
                block,
                lows[g],
                jnp.bfloat16 if last else jnp.float32,
            )
            parts.append(part)
        parts_down.append(functools.reduce(add, parts))
        if last:
            low_part = tensor_sum(jnp.concatenate(lows, axis=1), bits_below(shares)[:1])
        lows, back_gate = lax.optimization_barrier((lows, back_gate))
    by_rank = own_down.reshape(own, rank, width)
    rests = []
    for j in steps:
        for i in range(1, far):
            for k in range(1, near):
                start = ((plane // near + i) % far * near + (close + k) % near) * piece
                rest = lax.dynamic_slice_in_dim(by_rank, start, piece, 1)
                rests.append(shift(rest.reshape(own * piece, width), "adapter", j))

    def fold_start(part):
        half = part.shape[0] // near
        pieces_of = [
            lax.dynamic_slice_in_dim(part, ((close + j) % near) * half, half, 0)
            for j in range(near)
        ]
        return [pieces_of[0]] + [shift(pieces_of[j], "near", j) for j in range(1, near)]

    def fold_end(parts):
        return functools.reduce(add, parts)

    def send(part, axes):
        size = lax.axis_size(axes)
        return exchange(part.reshape(size, lot, part.shape[1]), axes)

    first = send(parts_down[0], ("near", "far", "tensor"))
    started = [fold_start(part) for part in parts_down[1:]]
    low_all = tensor_sum(low_part, bits_below(shares)[1:])
    base_share = scatter_columns(base_term, low_all)
    up_part = weight_product(
        low_all, row_slots, part_slots, part_select, scaled_of, (0, value_width), ADAPTER_SCALE
    )
    last_width = sum(part.shape[1] for part in parts_down[1:])
    up_start = fold_start(up_part)
    up_start, started, replies = lax.optimization_barrier((up_start, started, replies))
    back = sum(replies, back_all[:, :rank])
    folded = jnp.concatenate([fold_end(parts) for parts in started + [up_start]], axis=1)
    second = send(after(folded, first, base_share, *rests), ("far", "tensor"))
    arrived = [first, second]
    grad_down, grad_up = total_product(arrived, shares, width, last_width, value_width)
    grad_down = grad_down.reshape(stored, piece, shares * width)
    grad_up = grad_up.reshape(stored, piece, values)

    addends = [base_share]
    for j in steps:
        theirs = output_product(
            [],
            j,
            low_all,
            slot_columns,
            sent_slots[None, :],
            sent_select,
            own_ups,
        )
        addends.append(shift(theirs, "adapter", -j))
    downs = [own_down] + [block for n in range(len(steps)) for block in (
        quarters[n] + spread_far[n] + rests[n * per : (n + 1) * per]
    )]
    input_gradient = input_product(
        scaled,
        frozen_value_weight,
        back,
        slot_columns,
        columns,
        selects,
        downs,
        max(LANES, 1024 // sides),
    )
    addends[0] = after(addends[0], input_gradient)
    mixed_out = output_product(
        addends, 0, low_all, slot_columns, sent_slots[None, :], sent_select, own_ups
    )
    return mixed_out, input_gradient, grad_down, grad_up


def solution(mesh):
    planes = mesh.shape["dp"]
    near = 2 if planes % 2 == 0 else 1
    split = Mesh(
        mesh.devices.reshape((planes // near, near) + mesh.devices.shape[1:]),
        ("far", "near") + tuple(mesh.axis_names[1:]),
    )
    dp = ("far", "near")
    lines = dp + ("adapter",)
    return jax.shard_map(
        shards,
        mesh=split,
        in_specs=(
            P(lines, "tensor"),
            P("tensor", None),
            P(("adapter", "tensor"), None, None),
            P(("adapter", "tensor"), None, None),
            P(lines, None),
            P(lines),
            P(lines, None),
            P(),
        ),
        out_specs=(
            P(lines, "tensor"),
            P(lines, "tensor"),
            P(("adapter", "tensor"), dp, None),
            P(("adapter", "tensor"), dp, None),
        ),
        check_vma=False,
    )
```

```python
import functools

import jax
import jax.numpy as jnp
from jax import lax
from jax.experimental import pallas as pl
from jax.experimental.pallas import tpu as pltpu
from jax.sharding import Mesh
from jax.sharding import PartitionSpec as P

ADAPTER_SCALE = 0.5
PIECES = (2, 4, 4)
SPLIT = 128
HINT = 1000
LANES = 128
VMEM = 56 * 1024 * 1024


def exchange(pieces, axes):
    return lax.all_to_all(pieces, axes, split_axis=0, concat_axis=0, tiled=True)


def shift(array, axis, step):
    size = lax.axis_size(axis)
    return lax.ppermute(array, axis, [(i, (i + step) % size) for i in range(size)])


def swap(array, axis, bit):
    return lax.ppermute(array, axis, [(i, i ^ bit) for i in range(lax.axis_size(axis))])


def after(value, *earlier):
    return lax.optimization_barrier((value,) + earlier)[0]


def add(a, b):
    return (a.astype(jnp.float32) + b.astype(jnp.float32)).astype(jnp.bfloat16)


def bits_below(size):
    return [1 << i for i in range(size.bit_length() - 1)]


def tensor_sum(total, bits=None):
    for bit in bits_below(lax.axis_size("tensor")) if bits is None else bits:
        total = add(total, swap(total, "tensor", bit))
    return total


def scatter_columns(term, gate=None):
    size = lax.axis_size("tensor")
    share = lax.axis_index("tensor")
    width = term.shape[1] // size
    blocks = [
        lax.dynamic_slice_in_dim(term, (share ^ i) * width, width, 1) for i in range(size)
    ]
    for bit in bits_below(size):
        kept = [i for i in range(size) if i % (2 * bit) == 0]
        if 2 * bit == size:
            blocks = after(blocks, gate)
        got = swap(jnp.concatenate([blocks[i ^ bit] for i in kept], axis=1), "tensor", bit)
        for n, i in enumerate(kept):
            blocks[i] = add(blocks[i], got[:, n * width : (n + 1) * width])
    return blocks[0]


def dot(a, b, ca, cb):
    return lax.dot_general(a, b, (((ca,), (cb,)), ((), ())), preferred_element_type=jnp.float32)


def call(body, grid, in_specs, out_spec, out_shape, operands, flops, scratch=()):
    moved = sum(x.size * x.dtype.itemsize for x in operands)
    return pl.pallas_call(
        body,
        grid=grid,
        in_specs=in_specs,
        out_specs=out_spec,
        out_shape=out_shape,
        scratch_shapes=list(scratch),
        compiler_params=pltpu.CompilerParams(vmem_limit_bytes=VMEM),
        cost_estimate=pl.CostEstimate(flops=flops // HINT, bytes_accessed=moved // HINT, transcendentals=0),
    )(*operands)


def whole(array):
    return pl.BlockSpec(array.shape, lambda i: (0,) * array.ndim)


def fold_body(count, rank, scale, *refs):
    lines, weight, column_slots, slots = refs[:count], refs[count], refs[count + 1], refs[count + 2]
    out = refs[-1]
    step = max(rank, LANES)
    results = []
    for n in range(count):
        full = dot(lines[n][...], weight[...], 1, 1)
        full = jnp.where(slots[:, n : n + 1] == column_slots[...], full, 0.0)
        total = full[:, :step]
        for i in range(step, full.shape[1], step):
            total += full[:, i : i + step]
        results.append(sum(total[:, i : i + rank] for i in range(0, step, rank)))
    result = scale * jnp.concatenate(results, axis=1)
    if len(refs) == count + 5:
        result += refs[count + 3][...]
    out[...] = result.astype(out.dtype)


def fold_product(lines, weight, block, column_slots, slots, rank, scale, before, dtype):
    count = len(lines)
    rows = slots.shape[0]
    tile = rows // 2
    offset, depth = block
    specs = [
        pl.BlockSpec((tile, depth), functools.partial(lambda o, i: (i, o), 0))
        if line.shape[1] == depth
        else pl.BlockSpec((tile, depth), lambda i: (i, offset))
        for line in lines
    ]
    specs.append(pl.BlockSpec((weight.shape[0], depth), lambda i: (0, offset)))
    specs.append(whole(column_slots))
    specs.append(pl.BlockSpec((tile, count), lambda i: (i, 0)))
    operands = list(lines) + [weight, column_slots, slots]
    out_spec = pl.BlockSpec((tile, count * rank), lambda i: (i, 0))
    if before is not None:
        specs.append(out_spec)
        operands.append(before)
    return call(
        functools.partial(fold_body, count, rank, scale),
        (2,),
        specs,
        out_spec,
        jax.ShapeDtypeStruct((rows, count * rank), dtype),
        operands,
        2 * count * rows * weight.shape[0] * depth,
    )


def weight_body(count, rank, scale, *refs):
    compact, row_slots, column_slots, select = refs[:4]
    lines, out, spread = refs[4 : 4 + count], refs[-2], refs[-1]

    @pl.when(pl.program_id(0) == 0)
    def _():
        for n in range(count):
            wide = dot(select[...], compact[:, n * rank : (n + 1) * rank], 1, 1)
            mine = column_slots[...] == row_slots[n : n + 1, :]
            spread[n] = jnp.where(mine, wide, 0.0).astype(jnp.bfloat16)

    total = dot(spread[0], lines[0][...], 1, 0)
    for n in range(1, count):
        total += dot(spread[n], lines[n][...], 1, 0)
    out[...] = (scale * total).astype(out.dtype)


def weight_product(compact, row_slots, column_slots, select, lines, block, scale):
    count = len(lines)
    rows = row_slots.shape[1]
    columns, rank = select.shape
    offset, width = block
    tile = min(width, 512)
    per = width // tile
    specs = [whole(x) for x in (compact, row_slots, column_slots, select)]
    for line in lines:
        skip = 0 if line.shape[1] == width else offset * per
        specs.append(pl.BlockSpec((rows, tile), functools.partial(lambda s, i: (0, s + i), skip)))
    return call(
        functools.partial(weight_body, count, rank, scale),
        (per,),
        specs,
        pl.BlockSpec((columns, tile), lambda i: (0, i)),
        jax.ShapeDtypeStruct((columns, width), jnp.bfloat16),
        [compact, row_slots, column_slots, select] + list(lines),
        2 * count * rows * columns * width,
        [pltpu.VMEM((count, columns, rows), jnp.bfloat16)],
    )


def piece_body(count, rank, has_before, *refs):
    compact, row_slots, part_slots, select, weight, column_slots, slots = refs[:7]
    lines = refs[7 : 7 + count]
    out_weight, out_low, spread, *fulls = refs[7 + count + has_before :]
    step = pl.program_id(0)

    @pl.when(step == 0)
    def _():
        for n in range(count):
            wide = dot(select[...], compact[:, n * rank : (n + 1) * rank], 1, 1)
            mine = part_slots[...] == row_slots[n : n + 1, :]
            spread[n] = jnp.where(mine, wide, 0.0).astype(jnp.bfloat16)
            if fulls:
                fulls[n][...] = dot(lines[n][...], weight[...], 1, 1)

    if fulls:

        @pl.when(step > 0)
        def _():
            for n in range(count):
                fulls[n][...] += dot(lines[n][...], weight[...], 1, 1)

    @pl.when(step == pl.num_programs(0) - 1)
    def _():
        block = max(rank, LANES)
        results = []
        for n in range(count):
            full = fulls[n][...] if fulls else dot(lines[n][...], weight[...], 1, 1)
            full = jnp.where(slots[:, n : n + 1] == column_slots[...], full, 0.0)
            total = full[:, :block]
            for i in range(block, full.shape[1], block):
                total += full[:, i : i + block]
            results.append(sum(total[:, i : i + rank] for i in range(0, block, rank)))
        result = jnp.concatenate(results, axis=1)
        if has_before:
            result += refs[7 + count][...]
        out_low[...] = result.astype(out_low.dtype)

    total = dot(spread[0], lines[0][...], 1, 0)
    for n in range(1, count):
        total += dot(spread[n], lines[n][...], 1, 0)
    out_weight[...] = total.astype(out_weight.dtype)


def piece_product(
    compact, row_slots, part_slots, select, weight, column_slots, slots, lines, block, before, dtype
):
    count = len(lines)
    rows = row_slots.shape[1]
    columns, rank = select.shape
    offset, width = block
    tile = min(width, 512)
    per = width // tile
    here = lambda i: (0, offset * per + i)
    small = [compact, row_slots, part_slots, select, column_slots, slots]
    specs = [whole(x) for x in small[:4]] + [pl.BlockSpec((columns, tile), here)]
    specs += [whole(x) for x in small[4:]]
    for line in lines:
        skip = 0 if line.shape[1] == width else offset * per
        specs.append(pl.BlockSpec((rows, tile), functools.partial(lambda s, i: (0, s + i), skip)))
    operands = small[:4] + [weight] + small[4:] + list(lines)
    if before is not None:
        specs.append(whole(before))
        operands.append(before)
    low = jax.ShapeDtypeStruct((rows, count * rank), dtype)
    return call(
        functools.partial(piece_body, count, rank, before is not None),
        (per,),
        specs,
        [pl.BlockSpec((columns, tile), lambda i: (0, i)), whole(low)],
        [jax.ShapeDtypeStruct((columns, width), jnp.bfloat16), low],
        operands,
        4 * count * rows * columns * width,
        [pltpu.VMEM((count, columns, rows), jnp.bfloat16)]
        + [pltpu.VMEM((rows, columns), jnp.float32)] * (count if per > 1 else 0),
    )


def input_body(count, *refs):
    scaled, frozen, compact, slots = refs[:4]
    columns, selects, downs = (refs[4 + i * count : 4 + (i + 1) * count] for i in range(3))
    out, spreads = refs[-1 - count], refs[-count:]

    @pl.when(pl.program_id(0) == 0)
    def _():
        for n in range(count):
            wide = dot(compact[...], selects[n][...], 1, 0)
            mine = slots[:, :1] == columns[n][...]
            spreads[n][...] = jnp.where(mine, wide, 0.0).astype(jnp.bfloat16)

    total = dot(scaled[...], frozen[...], 1, 1)
    for n in range(count):
        total += dot(spreads[n][...], downs[n][...], 1, 0)
    out[...] = total.astype(out.dtype)


def input_product(scaled, frozen, compact, slots, columns, selects, downs, tile):
    count = len(downs)
    rows, values = scaled.shape
    width = downs[0].shape[1]
    specs = [whole(scaled), pl.BlockSpec((tile, values), lambda i: (i, 0))]
    specs += [whole(x) for x in [compact, slots] + columns + selects]
    specs += [pl.BlockSpec((x.shape[0], tile), lambda i: (0, i)) for x in downs]
    return call(
        functools.partial(input_body, count),
        (width // tile,),
        specs,
        pl.BlockSpec((rows, tile), lambda i: (0, i)),
        jax.ShapeDtypeStruct((rows, width), jnp.bfloat16),
        [scaled, frozen, compact, slots] + columns + selects + list(downs),
        2 * rows * width * (values + sum(x.shape[0] for x in downs)),
        [pltpu.VMEM((rows, x.shape[0]), jnp.bfloat16) for x in downs],
    )


def output_body(count, which, rank, *refs):
    compact, slots, column_slots, select, ups = refs[count : count + 5]
    out = refs[-1]
    wide = dot(compact[:, which * rank : (which + 1) * rank], select[...], 1, 0)
    mine = slots[:, which : which + 1] == column_slots[...]
    spread = jnp.where(mine, wide, 0.0).astype(jnp.bfloat16)
    result = ADAPTER_SCALE * dot(spread, ups[...], 1, 0)
    for addend in refs[:count]:
        result += addend[...].astype(jnp.float32)
    out[...] = result.astype(out.dtype)


def output_product(addends, which, compact, slots, column_slots, select, ups):
    rows, width = compact.shape[0], ups.shape[1]
    tile = rows // 2
    line = lambda i: (i, 0)
    operands = list(addends) + [compact, slots]
    specs = [pl.BlockSpec((tile, x.shape[1]), line) for x in operands]
    operands += [column_slots, select, ups]
    specs += [whole(x) for x in operands[-3:]]
    return call(
        functools.partial(output_body, len(addends), which, select.shape[0]),
        (rows // tile,),
        specs,
        pl.BlockSpec((tile, width), line),
        jax.ShapeDtypeStruct((rows, width), jnp.bfloat16),
        operands,
        2 * rows * width * ups.shape[0],
    )


def total_body(shares, width, last_width, value_width, *refs):
    out_down, out_up = refs[-2:]
    position = 0
    for ref in refs[:-2]:
        last = ref is refs[-3]
        columns = last_width if last else ref.shape[2]
        for share in range(shares):
            total = sum(
                ref[source].astype(jnp.float32) for source in range(share, ref.shape[0], shares)
            )
            start = share * width + position
            out_down[:, start : start + columns] = total[:, :columns].astype(jnp.bfloat16)
            if last:
                start = share * value_width
                out_up[:, start : start + value_width] = total[:, columns:].astype(jnp.bfloat16)
        position += columns


def total_product(arrived, shares, width, last_width, value_width):
    lot = arrived[0].shape[1]
    shapes = [
        jax.ShapeDtypeStruct((lot, shares * columns), jnp.bfloat16)
        for columns in (width, value_width)
    ]
    return call(
        functools.partial(total_body, shares, width, last_width, value_width),
        (1,),
        [whole(x) for x in arrived],
        [whole(x) for x in shapes],
        shapes,
        arrived,
        1000,
    )


def choose(ranks, rank):
    return (jnp.arange(rank, dtype=jnp.int32)[:, None] == ranks[None, :]).astype(jnp.bfloat16)


def shards(
    tokens,
    frozen_value_weight,
    adapter_down_weight,
    adapter_up_weight,
    cotangent,
    language_pair_index,
    language_pair_counts,
    adapter_owner_table,
):
    sides = lax.axis_size("adapter")
    shares = lax.axis_size("tensor")
    far, near = lax.axis_size("far"), lax.axis_size("near")
    planes = far * near
    side = lax.axis_index("adapter")
    share = lax.axis_index("tensor")
    plane = lax.axis_index(("far", "near"))
    close = lax.axis_index("near")
    rows, width = tokens.shape
    stored, rank, _ = adapter_down_weight.shape
    values = cotangent.shape[1]
    value_width = values // shares
    own = shares * stored
    piece = rank // planes
    lot = stored * piece
    steps = range(1, sides)

    quarter = lax.dynamic_slice_in_dim(adapter_down_weight, plane * piece, piece, 1)
    quarter = quarter.reshape(lot, shares * width)
    parcel = jnp.stack([quarter[:, s * width : (s + 1) * width] for s in range(shares)])
    parcel = jnp.broadcast_to(parcel[None], (sides,) + parcel.shape)
    parcel = parcel.reshape(sides * shares, lot, width)
    got = exchange(parcel, ("adapter", "tensor"))

    quarters = []
    for j in steps:
        block = lax.dynamic_slice(
            got, (((side - j) % sides) * shares, 0, 0), (shares, lot, width)
        ).reshape(own * piece, width)
        quarters.append([block] + [shift(block, "near", i) for i in range(1, near)])
    shared = [block for blocks in quarters for block in blocks]
    spread_far = [[shift(q[0], "far", i) for i in range(1, far)] for q in quarters]

    pairs = jnp.arange(adapter_owner_table.shape[0], dtype=jnp.int32)
    matches = language_pair_index[:, None] == pairs[None, :]
    slots = jnp.sum(jnp.where(matches, adapter_owner_table[None, :], 0), axis=1)
    row_counts = jnp.sum(jnp.where(matches, language_pair_counts[0][None, :], 0), axis=1)
    row_weight = 1.0 / row_counts.astype(jnp.float32)
    scaled = (cotangent.astype(jnp.float32) * row_weight[:, None]).astype(jnp.bfloat16)
    scaled_part = lax.dynamic_slice_in_dim(scaled, share * value_width, value_width, 1)

    tag_rows = -(-rows // value_width)
    tags = jnp.pad(slots, (0, tag_rows * value_width - rows)).reshape(tag_rows, value_width)
    tags = jnp.concatenate([tags // SPLIT, tags % SPLIT]).astype(jnp.bfloat16)
    tags = jnp.pad(tags, ((0, -2 * tag_rows % 16), (0, 0)))
    message = after(jnp.concatenate([scaled_part, tags]), parcel)
    scaled_of, slots_of = [scaled_part], [slots]
    for j in steps:
        answer = shift(message, "adapter", j)
        scaled_of.append(answer[:rows])
        numbers = answer[rows : rows + 2 * tag_rows].astype(jnp.int32)
        numbers = numbers[:tag_rows] * SPLIT + numbers[tag_rows:]
        slots_of.append(numbers.reshape(-1)[:rows])
    row_slots = jnp.stack(slots_of)
    slot_columns = row_slots.T

    def over_shares(matrix):
        columns = matrix.shape[1] // shares
        sent = [
            lax.dynamic_slice_in_dim(matrix, (share ^ k) * columns, columns, 1)
            for k in range(shares)
        ]
        return jnp.concatenate(
            [sent[0]] + [swap(sent[k], "tensor", k) for k in range(1, shares)]
        )

    own_ups = over_shares(adapter_up_weight.reshape(stored * rank, values))
    down_flat = after(adapter_down_weight.reshape(stored * rank, shares * width), own_ups)
    own_down = over_shares(down_flat)
    gated_ups = after(own_ups, got)

    pieces, position = [], 0
    for part in PIECES:
        piece_width = width // part
        others = tokens[:, position : position + piece_width]
        others = after(others, own_ups)
        pieces.append(
            (
                (position // piece_width, piece_width),
                [tokens] + [shift(others, "adapter", j) for j in steps],
            )
        )
        position += piece_width

    base_term = dot(tokens, frozen_value_weight, 1, 0).astype(jnp.bfloat16)

    column = jnp.arange(own * rank, dtype=jnp.int32)
    sent_slots = (side * shares + (share ^ (column // (stored * rank)))) * stored
    sent_slots += (column // rank) % stored
    sent_select = choose(column % rank, rank)
    part_local = (column % (own * piece)) // piece
    part_plane = column // (own * piece)
    part_plane = (part_plane % far) * near + part_plane // far
    part_ranks = part_plane * piece + column % piece
    part_slots = (side * own + part_local)[:, None]
    part_select = choose(part_ranks, rank).T

    columns, selects = [sent_slots[None, :]], [sent_select]
    quarter_column = column[: own * piece]
    adapter = quarter_column // piece
    per = (far - 1) * (near - 1)
    for j in steps:
        away = (side - j) % sides
        mine = plane // near
        stored_order = away * own + adapter
        sent_order = (away * shares + (share ^ (adapter // stored))) * stored + adapter % stored
        blocks = [(stored_order, mine * near + (close - i) % near) for i in range(near)]
        blocks += [(stored_order, (mine - i) % far * near + close) for i in range(1, far)]
        blocks += [
            (sent_order, (mine + i) % far * near + (close + k) % near)
            for i in range(1, far)
            for k in range(1, near)
        ]
        for block_slots, from_plane in blocks:
            columns.append(block_slots[None, :])
            selects.append(choose(from_plane * piece + quarter_column % piece, rank))
    tables = (part_slots, part_select, sent_slots, sent_select, columns, selects, slot_columns)
    gated_ups, tables = lax.optimization_barrier((gated_ups, tables))
    part_slots, part_select, sent_slots, sent_select, columns, selects, slot_columns = tables

    back_part = fold_product(
        scaled_of,
        gated_ups,
        (0, value_width),
        sent_slots[None, :],
        slot_columns,
        rank,
        ADAPTER_SCALE,
        None,
        jnp.bfloat16,
    )
    back_part, base_term = lax.optimization_barrier((back_part, base_term))
    far_blocks = [block for blocks in spread_far for block in blocks]
    back_part = after(back_part, own_down, *shared, *far_blocks, *pieces[0][1][1:])
    back_all = tensor_sum(back_part)
    replies = [shift(back_all[:, j * rank : (j + 1) * rank], "adapter", -j) for j in steps]


    back_gate = back_all
    groups = [slice(g, min(g + 2, sides)) for g in range(0, sides, 2)]
    lows = [None] * len(groups)
    parts_down = []
    for n, (block, lines) in enumerate(pieces):
        last = n == len(pieces) - 1
        parts = []
        for g, group in enumerate(groups):
            part, lows[g] = piece_product(
                back_gate[:, group.start * rank : group.stop * rank],
                row_slots[group],
                part_slots,
                part_select,
                own_down,
                sent_slots[None, :],
                slot_columns[:, group],
                lines[group],
                block,
                lows[g],
                jnp.bfloat16 if last else jnp.float32,
            )
            parts.append(part)
        parts_down.append(functools.reduce(add, parts))
        if last:
            low_part = tensor_sum(jnp.concatenate(lows, axis=1), bits_below(shares)[1:])
        lows, back_gate = lax.optimization_barrier((lows, back_gate))
    by_rank = own_down.reshape(own, rank, width)
    rests = []
    for j in steps:
        for i in range(1, far):
            for k in range(1, near):
                start = ((plane // near + i) % far * near + (close + k) % near) * piece
                rest = lax.dynamic_slice_in_dim(by_rank, start, piece, 1)
                rests.append(shift(rest.reshape(own * piece, width), "adapter", j))

    def fold_start(part):
        half = part.shape[0] // near
        pieces_of = [
            lax.dynamic_slice_in_dim(part, ((close + j) % near) * half, half, 0)
            for j in range(near)
        ]
        return [pieces_of[0]] + [shift(pieces_of[j], "near", j) for j in range(1, near)]

    def fold_end(parts):
        return functools.reduce(add, parts)

    def send(part, axes):
        size = lax.axis_size(axes)
        return exchange(part.reshape(size, lot, part.shape[1]), axes)

    first = send(parts_down[0], ("near", "far", "tensor"))
    started = [fold_start(part) for part in parts_down[1:]]
    low_all = tensor_sum(low_part, bits_below(shares)[:1])
    base_share = scatter_columns(base_term, low_all)
    up_part = weight_product(
        low_all, row_slots, part_slots, part_select, scaled_of, (0, value_width), ADAPTER_SCALE
    )
    last_width = sum(part.shape[1] for part in parts_down[1:])
    up_start = fold_start(up_part)
    up_start, started, replies = lax.optimization_barrier((up_start, started, replies))
    back = sum(replies, back_all[:, :rank])
    folded = jnp.concatenate([fold_end(parts) for parts in started + [up_start]], axis=1)
    second = send(after(folded, first, base_share, *rests), ("far", "tensor"))
    arrived = [first, second]
    grad_down, grad_up = total_product(arrived, shares, width, last_width, value_width)
    grad_down = grad_down.reshape(stored, piece, shares * width)
    grad_up = grad_up.reshape(stored, piece, values)

    addends = [base_share]
    for j in steps:
        theirs = output_product(
            [],
            j,
            low_all,
            slot_columns,
            sent_slots[None, :],
            sent_select,
            own_ups,
        )
        addends.append(shift(theirs, "adapter", -j))
    downs = [own_down] + [block for n in range(len(steps)) for block in (
        quarters[n] + spread_far[n] + rests[n * per : (n + 1) * per]
    )]
    input_gradient = input_product(
        scaled,
        frozen_value_weight,
        back,
        slot_columns,
        columns,
        selects,
        downs,
        max(LANES, 1024 // sides),
    )
    addends[0] = after(addends[0], input_gradient)
    mixed_out = output_product(
        addends, 0, low_all, slot_columns, sent_slots[None, :], sent_select, own_ups
    )
    return mixed_out, input_gradient, grad_down, grad_up


def solution(mesh):
    planes = mesh.shape["dp"]
    near = 2 if planes % 2 == 0 else 1
    split = Mesh(
        mesh.devices.reshape((planes // near, near) + mesh.devices.shape[1:]),
        ("far", "near") + tuple(mesh.axis_names[1:]),
    )
    dp = ("far", "near")
    lines = dp + ("adapter",)
    return jax.shard_map(
        shards,
        mesh=split,
        in_specs=(
            P(lines, "tensor"),
            P("tensor", None),
            P(("adapter", "tensor"), None, None),
            P(("adapter", "tensor"), None, None),
            P(lines, None),
            P(lines),
            P(lines, None),
            P(),
        ),
        out_specs=(
            P(lines, "tensor"),
            P(lines, "tensor"),
            P(("adapter", "tensor"), dp, None),
            P(("adapter", "tensor"), dp, None),
        ),
        check_vma=False,
    )
```
